32 devices in a mesh: dp: 8 (over z, y), mp: 4 (over x, core).
Axes of the slice: x: 2, y: 2, z: 4, core: 2. Of those that a mesh axis runs over, the one named last changes fastest.
Arguments:
- tokens: bfloat16 [1024, 16384], P('dp', 'mp'), may hold values from -6 to 6
- cotangent: bfloat16 [1024, 16384], P('dp', 'mp'), may hold values from -6 to 6
- up_right: bfloat16 [2, 128, 128, 128], P(None, 'mp'), may hold values from -0.5 to 0.5
- up_left: bfloat16 [2, 128, 128, 128], P(None, 'mp'), may hold values from -0.5 to 0.5
- down_first_factor: bfloat16 [2, 128, 128, 128], P(None, 'mp'), may hold values from -0.5 to 0.5
- down_left: bfloat16 [2, 128, 128, 128], P(None, 'mp'), may hold values from -0.5 to 0.5
Outputs:
- mixed: bfloat16 [1024, 16384], P('dp', 'mp')
- tokens_grad: bfloat16 [1024, 16384], P('dp', 'mp')
- grad_up_right: float32 [2, 128, 128, 128], P(None, 'mp', 'dp')
- grad_up_left: float32 [2, 128, 128, 128], P(None, 'mp', 'dp')
- grad_down_right: float32 [2, 128, 128, 128], P(None, 'mp', 'dp')
- grad_down_left: float32 [2, 128, 128, 128], P(None, 'mp', 'dp')
The draws below stay inside these ranges and needn't reach their ends.
All inputs are finite; a program needn't handle non-finite values.
Results may differ from the reference program's by a relative error of at most 0.01.
Values may be sent and summed in bfloat16 or wider, within the bound.
A program may use at most 128 MiB of HBM per device.

```python
import jax
import jax.numpy as jnp
from jax import lax

D = 16384
BLK = 128
NB = 128
Q = 2
TOKENS = 1024
N_DP = 8


def block_scale(key, extent, pieces, smallest, top_value):
    def one(dim, shards_of):
        draws = jax.random.uniform(jax.random.fold_in(jax.random.fold_in(key, 6), dim), (shards_of,), jnp.float32, smallest / len(pieces), top_value / len(pieces))
        return jnp.repeat(jnp.exp(draws), extent[dim] // shards_of).reshape((-1,) + (1,) * (len(extent) - dim - 1))

    gain = one(*pieces[0])
    for cut in pieces[1:]:
        gain = gain * one(*cut)
    return gain


def noise(key, extent, width, bound, shards=(), dtype=jnp.bfloat16):
    result = width * jax.random.normal(key, extent, jnp.float32)
    if shards:
        result = result * block_scale(key, extent, shards, -0.22, 0.18)
    return jnp.clip(result, -bound, bound).astype(dtype)


def setup_inputs(seed: int = 0) -> dict:
    streams_of = jax.random.split(jax.random.key(seed), 7)
    tokens = noise(streams_of[0], (TOKENS, D), 1.0, 6.0, ((0, 8), (1, 4)))
    cotangent = noise(streams_of[1], (TOKENS, D), 1.0, 6.0, ((0, 8), (1, 4)))
    up_right = noise(streams_of[2], (Q, NB, BLK, BLK), BLK ** -0.5, 0.5, ((1, 4),))
    up_left = noise(streams_of[3], (Q, NB, NB, BLK), NB ** -0.5, 0.5, ((1, 4),))
    down_first_factor = noise(streams_of[4], (Q, NB, BLK, BLK), BLK ** -0.5, 0.5, ((1, 4),))
    down_left = noise(streams_of[5], (Q, NB, NB, BLK), NB ** -0.5, 0.5, ((1, 4),))
    return dict(tokens=tokens, cotangent=cotangent, up_right=up_right, up_left=up_left, down_first_factor=down_first_factor, down_left=down_left)


gelu_root = 0.7978845608
gelu_cube = 0.044715


def gelu_value(pre_values):
    inner_arg = gelu_root * (pre_values + gelu_cube * pre_values * pre_values * pre_values)
    return 0.5 * pre_values * (1.0 + jnp.tanh(inner_arg))


def gelu_slope(pre_values):
    inner_arg = gelu_root * (pre_values + gelu_cube * pre_values * pre_values * pre_values)
    tanh_term = jnp.tanh(inner_arg)
    return 0.5 * (1.0 + tanh_term) + 0.5 * pre_values * (1.0 - tanh_term * tanh_term) * gelu_root * (1.0 + 3.0 * gelu_cube * pre_values * pre_values)


def shard_partials(einsum_form, first_arr, second_arr):
    first_split = first_arr.reshape((N_DP, TOKENS // N_DP) + first_arr.shape[1:])
    second_split = second_arr.reshape((N_DP, TOKENS // N_DP) + second_arr.shape[1:])
    partial_terms = jnp.einsum(einsum_form, first_split, second_split)
    rounded = lax.optimization_barrier(partial_terms.astype(jnp.bfloat16))
    return jnp.sum(rounded.astype(jnp.float32), axis=0) * (TOKENS ** -0.5)


def reference(tokens, cotangent, up_right, up_left, down_first_factor, down_left):
    blocked_in = tokens.reshape(TOKENS, NB, BLK).astype(jnp.float32)
    upstream = cotangent.reshape(TOKENS, NB, BLK).astype(jnp.float32)
    out_acc = jnp.zeros((TOKENS, NB, BLK), jnp.float32)
    grad_acc = jnp.zeros((TOKENS, NB, BLK), jnp.float32)
    list_ur, list_ul, list_dr, list_dl = [], [], [], []
    for fourth_part in range(Q):
        weight_ur = up_right[fourth_part].astype(jnp.float32)
        up_left_weight = up_left[fourth_part].astype(jnp.float32)
        weight_dr = down_first_factor[fourth_part].astype(jnp.float32)
        weight_dl = down_left[fourth_part].astype(jnp.float32)
        right_factor_output = jnp.einsum("tij,ijc->tic", blocked_in, weight_ur).astype(jnp.bfloat16).astype(jnp.float32)
        preactivation_values = jnp.einsum("fuh,hul->fhl", right_factor_output, up_left_weight)
        hidden = gelu_value(preactivation_values).astype(jnp.bfloat16).astype(jnp.float32)
        down_panel = jnp.einsum("tca,cae->tce", hidden, weight_dr).astype(jnp.bfloat16).astype(jnp.float32)
        out_acc = out_acc + jnp.einsum("tce,ecf->tef", down_panel, weight_dl)
        list_dl.append(shard_partials("stce,stef->secf", down_panel, upstream))
        down_grad = jnp.einsum("tef,ecf->tce", upstream, weight_dl).astype(jnp.bfloat16).astype(jnp.float32)
        hidden_grad = jnp.einsum("tce,cae->tca", down_grad, weight_dr)
        list_dr.append(shard_partials("stca,stce->scae", hidden, down_grad))
        preactivation_gradient = (hidden_grad * gelu_slope(preactivation_values)).astype(jnp.bfloat16).astype(jnp.float32)
        list_ul.append(shard_partials("stac,stcb->scab", right_factor_output, preactivation_gradient))
        right_factor_gradient = jnp.einsum("gdw,dsw->gsd", preactivation_gradient, up_left_weight).astype(jnp.bfloat16).astype(jnp.float32)
        list_ur.append(shard_partials("stij,stic->sijc", blocked_in, right_factor_gradient))
        grad_acc = grad_acc + jnp.einsum("tic,ijc->tij", right_factor_gradient, weight_ur)
    mixed = out_acc.reshape(TOKENS, D).astype(jnp.bfloat16)
    tokens_grad = grad_acc.reshape(TOKENS, D).astype(jnp.bfloat16)
    return (mixed, tokens_grad, jnp.stack(list_ur), jnp.stack(list_ul), jnp.stack(list_dr), jnp.stack(list_dl))
```

```python
import functools

import jax
import jax.numpy as jnp
from jax import lax
from jax.experimental import pallas as pl
from jax.experimental.pallas import tpu as pltpu
from jax.sharding import PartitionSpec as P

gelu_root = 0.7978845608
gelu_cube = 0.044715
F32 = jnp.float32
BF16 = jnp.bfloat16


def mm(lhs, rhs, ldim, rdim):
    return lax.dot_general(lhs, rhs, (((ldim,), (rdim,)), ((), ())), preferred_element_type=F32)


def send_panel(outs, kind, scratch, me, blocks):
    span = blocks * blocks
    for k, out in enumerate(outs):
        start = pl.multiple_of((me ^ k) * span, span)
        rows = scratch[pl.ds(start, span), :]
        out[kind] = rows.reshape(out.shape[1:]).astype(BF16)


def gather_rows(parts, kind, scratch, slot, me, block, blocks):
    for k, part in enumerate(parts):
        start = pl.multiple_of((me ^ k) * blocks, blocks)
        scratch[slot, pl.ds(start, blocks), :] = part[kind, block].astype(F32)
    return scratch[slot].astype(BF16)


def hop_order(ways, kind):
    bits = [1 << b for b in range(ways.bit_length() - 1)]
    return [bits[1], bits[0]] + bits[2:] if kind and len(bits) > 1 else bits


def store_grad(outs, kind, block, value, scratch, slot, me, ways):
    rows = value.shape[0] // ways
    first, *later = hop_order(ways, kind)
    scratch[slot] = value
    for p in range(ways // 2):
        rel = sum(bit for t, bit in enumerate(later) if p >> t & 1)
        for out, target in ((outs[2 * kind], rel), (outs[2 * kind + 1], rel + first)):
            start = pl.multiple_of((me ^ target) * rows, rows)
            out[p, block] = scratch[slot, pl.ds(start, rows), :].astype(BF16)


def panels_kernel(ways, me_ref, x_ref, g_ref, ur_ref, dl_ref, *rest):
    outs, scr_r, scr_b = rest[:ways], rest[ways], rest[ways + 1]
    blocks, width = ur_ref.shape[1], ur_ref.shape[2]
    me = me_ref[0]
    for i in range(blocks):
        cols = slice(i * width, (i + 1) * width)
        scr_r[pl.ds(i, width, stride=blocks), :] = mm(ur_ref[0, i], x_ref[:, cols], 0, 1)
        scr_b[pl.ds(i, width, stride=blocks), :] = mm(dl_ref[0, i], g_ref[:, cols], 1, 1)
    send_panel(outs, 0, scr_r, me, blocks)
    send_panel(outs, 1, scr_b, me, blocks)


def full_spec(shape):
    return pl.BlockSpec(shape, lambda s: (0,) * len(shape))


def group_spec(w, q):
    return pl.BlockSpec((1,) + w.shape[1:], lambda s: (q, 0, 0, 0))


def limits(flops, mib):
    return dict(
        compiler_params=pltpu.CompilerParams(vmem_limit_bytes=40 * 2**20),
        cost_estimate=pl.CostEstimate(flops=flops * 8, bytes_accessed=mib * 2**20, transcendentals=0),
    )


def make_panels(me, x, g, ur, dl, q, ways):
    tok, blocks, width = x.shape[0], ur.shape[1], ur.shape[2]
    part = jax.ShapeDtypeStruct((2, blocks, blocks, tok), BF16)
    return pl.pallas_call(
        functools.partial(panels_kernel, ways),
        out_shape=[part] * ways,
        grid=(1,),
        in_specs=[
            pl.BlockSpec(memory_space=pltpu.SMEM),
            full_spec(x.shape),
            full_spec(g.shape),
            group_spec(ur, q),
            group_spec(dl, q),
        ],
        out_specs=[full_spec(part.shape)] * ways,
        scratch_shapes=[pltpu.VMEM((width * blocks, tok), F32)] * 2,
        **limits(4 * tok * blocks * width * width, 8),
    )(me, x, g, ur, dl)


UNROLL = 4


def middle_kernel(mp_ways, dp_ways, me_ref, ul_ref, df_ref, *rest):
    n = mp_ways
    first_in, outs, grads = rest[:n], rest[n : 2 * n], rest[2 * n : 2 * n + 4]
    scr_d, scr_u, asm_r, asm_b, gr1, gr2 = rest[2 * n + 4 :]
    blocks, width = ul_ref.shape[1], ul_ref.shape[2]
    me_mp, me_dp = me_ref[0], me_ref[1]

    def one(c, slot):
        ul, df = ul_ref[0, c], df_ref[0, c]
        cu = gather_rows(first_in, 0, asm_r, slot, me_mp, c, blocks)
        dg = gather_rows(first_in, 1, asm_b, slot, me_mp, c, blocks)
        pre = mm(ul, cu, 0, 0)
        sq = pre * pre
        th = jnp.tanh(gelu_root * (pre + gelu_cube * sq * pre))
        half = 0.5 * (1.0 + th)
        hidden = (pre * half).astype(BF16)
        slope = half + 0.5 * pre * (1.0 - th * th) * (gelu_root * (1.0 + 3.0 * gelu_cube * sq))
        scr_d[pl.ds(c, width, stride=blocks), :] = mm(df, hidden, 0, 0)
        pg = (mm(df, dg, 1, 0) * slope).astype(BF16)
        scr_u[pl.ds(c, width, stride=blocks), :] = mm(ul, pg, 1, 0)
        store_grad(grads, 0, c, mm(hidden, dg, 1, 1), gr1, slot, me_dp, dp_ways)
        store_grad(grads, 1, c, mm(cu, pg, 1, 1), gr2, slot, me_dp, dp_ways)

    def step(s, carry):
        for slot in range(UNROLL):
            one(s * UNROLL + slot, slot)
        return carry

    lax.fori_loop(0, blocks // UNROLL, step, 0)
    send_panel(outs, 0, scr_d, me_mp, blocks)
    send_panel(outs, 1, scr_u, me_mp, blocks)


def grad_halves(blocks, width, dp_ways):
    return jax.ShapeDtypeStruct((dp_ways // 2, blocks, width // dp_ways, width), BF16)


def make_middle(me, first_in, ul, df, q, dp_ways):
    n = len(first_in)
    part = jax.ShapeDtypeStruct(first_in[0].shape, BF16)
    blocks, width, tok = ul.shape[1], ul.shape[2], part.shape[3]
    half = grad_halves(blocks, width, dp_ways)
    res = pl.pallas_call(
        functools.partial(middle_kernel, n, dp_ways),
        out_shape=[part] * n + [half] * 4,
        grid=(1,),
        in_specs=[pl.BlockSpec(memory_space=pltpu.SMEM)] + [group_spec(ul, q)] * 2 + [full_spec(part.shape)] * n,
        out_specs=[full_spec(part.shape)] * n + [full_spec(half.shape)] * 4,
        scratch_shapes=[pltpu.VMEM((width * blocks, tok), F32)] * 2
        + [pltpu.VMEM((UNROLL, width, tok), F32)] * 2
        + [pltpu.VMEM((UNROLL, width, width), F32)] * 2,
        **limits(12 * tok * blocks * width * width, 8),
    )(me, ul, df, *first_in)
    return res[:n], res[n:]


def last_grads_kernel(mp_ways, dp_ways, me_ref, x_ref, g_ref, *rest):
    n = mp_ways
    second_in, grads = rest[:n], rest[n : n + 4]
    asm_d, asm_u, gr1, gr2 = rest[n + 4 :]
    blocks = second_in[0].shape[1]
    width = gr1.shape[1]
    me_mp, me_dp = me_ref[0], me_ref[1]
    for e in range(blocks):
        cols = slice(e * width, (e + 1) * width)
        slot = e % UNROLL
        cd = gather_rows(second_in, 0, asm_d, slot, me_mp, e, blocks)
        rg = gather_rows(second_in, 1, asm_u, slot, me_mp, e, blocks)
        store_grad(grads, 0, e, mm(cd, g_ref[:, cols], 1, 0), gr1, slot, me_dp, dp_ways)
        store_grad(grads, 1, e, mm(rg, x_ref[:, cols], 1, 0).T, gr2, slot, me_dp, dp_ways)


def make_last_grads(me, second_in, x, g, width, dp_ways):
    n = len(second_in)
    part = second_in[0]
    blocks, tok = part.shape[1], part.shape[3]
    half = grad_halves(blocks, width, dp_ways)
    return pl.pallas_call(
        functools.partial(last_grads_kernel, n, dp_ways),
        out_shape=[half] * 4,
        grid=(1,),
        in_specs=[pl.BlockSpec(memory_space=pltpu.SMEM)] + [full_spec(x.shape)] * 2 + [full_spec(part.shape)] * n,
        out_specs=[full_spec(half.shape)] * 4,
        scratch_shapes=[pltpu.VMEM((UNROLL, width, tok), F32)] * 2 + [pltpu.VMEM((UNROLL, width, width), F32)] * 2,
        **limits(4 * tok * blocks * width * width, 6),
    )(me, x, g, *second_in)


def outputs_kernel(mp_ways, me_ref, dl_ref, ur_ref, *rest):
    n = mp_ways
    groups = dl_ref.shape[0]
    second_in = rest[: groups * n]
    mixed, tgrad, asm_d, asm_u = rest[groups * n :]
    blocks, width = dl_ref.shape[1], dl_ref.shape[2]
    me_mp = me_ref[0]
    for e in range(blocks):
        cols = slice(e * width, (e + 1) * width)
        out_sum = grad_sum = None
        for q in range(groups):
            parts = second_in[q * n : (q + 1) * n]
            slot = (e * groups + q) % UNROLL
            cd = gather_rows(parts, 0, asm_d, slot, me_mp, e, blocks)
            rg = gather_rows(parts, 1, asm_u, slot, me_mp, e, blocks)
            one = mm(cd, dl_ref[q, e], 0, 0)
            two = mm(ur_ref[q, e], rg, 1, 0)
            out_sum = one if q == 0 else out_sum + one
            grad_sum = two if q == 0 else grad_sum + two
        mixed[:, cols] = out_sum.astype(BF16)
        tgrad[:, cols] = grad_sum.T.astype(BF16)


def make_outputs(me, second_in, dl, ur):
    n = len(second_in[0])
    part = second_in[0][0]
    groups, blocks, width, tok = dl.shape[0], dl.shape[1], dl.shape[2], part.shape[3]
    out = jax.ShapeDtypeStruct((tok, blocks * width), BF16)
    return pl.pallas_call(
        functools.partial(outputs_kernel, n),
        out_shape=[out] * 2,
        grid=(1,),
        in_specs=[pl.BlockSpec(memory_space=pltpu.SMEM)]
        + [full_spec(dl.shape)] * 2
        + [full_spec(part.shape)] * (n * groups),
        out_specs=[full_spec(out.shape)] * 2,
        scratch_shapes=[pltpu.VMEM((UNROLL, width, tok), F32)] * 2,
        **limits(8 * tok * blocks * width * width, 10),
    )(me, dl, ur, *[p for parts in second_in for p in parts])


def xor_permute(array, axis, k):
    return lax.ppermute(array, axis, [(i, i ^ k) for i in range(lax.axis_size(axis))])


def exchange(parts):
    return [p if k == 0 else xor_permute(p, "mp", k) for k, p in enumerate(parts)]


def halving_rounds(reductions, scale):
    ways = lax.axis_size("dp")
    orders = [hop_order(ways, kind) for kind in range(2)]
    hops = len(orders[0])
    pairs = [[[h[0], h[1]], [h[2], h[3]]] for h in reductions]
    sums = [[None, None] for _ in reductions]
    for turn in range(hops + len(reductions) - 1):
        active = [(s, kind) for s in range(len(reductions)) if 0 <= turn - s < hops for kind in range(2)]
        got = [xor_permute(pairs[s][kind][1], "dp", orders[kind][turn - s]) for s, kind in active]
        got = lax.optimization_barrier(got)
        for (s, kind), arrived in zip(active, got):
            total = pairs[s][kind][0].astype(F32) + arrived.astype(F32)
            if total.shape[0] == 1:
                sums[s][kind] = total[0] * scale
                continue
            total = total.astype(BF16).reshape((total.shape[0] // 2, 2) + total.shape[1:])
            pairs[s][kind] = [total[:, 0], total[:, 1]]
    return sums


CHUNK = 8
MESH_IDS = pl.DeviceIdType.MESH


def flip(v):
    return 1 - v


def fused_kernel(
    mp_ways,
    x_in,
    g_in,
    ur_in,
    ul_in,
    df_in,
    dl_in,
    mixed_out,
    tgrad_out,
    gur_out,
    gul_out,
    gdf_out,
    gdl_out,
    x,
    g,
    ur,
    ul,
    df,
    dl,
    scr0,
    scr1,
    stage,
    land,
    part,
    got1,
    got2,
    got3,
    fin,
    acc_m,
    acc_t,
    out_m,
    out_t,
    in_sem,
    send_sem,
    recv_sem,
    hop_send,
    hop_recv,
    out_sem,
):
    groups, blocks, width = ur.shape[0], ur.shape[1], ur.shape[2]
    tok = x.shape[0]
    chunks = blocks // CHUNK
    rows = width // 8
    span = blocks * blocks
    steps = 2 * groups * chunks
    mid_steps = groups * chunks
    scale = (8 * tok) ** (-0.5)
    me, dp = lax.axis_index("mp"), lax.axis_index("dp")
    yb, zb, wb = dp % 2, (dp // 2) % 2, dp // 4

    def mp_peer(k):
        total = 0
        for b in range(mp_ways.bit_length() - 1):
            bit = (me // (1 << b)) % 2
            total = total + (flip(bit) if k >> b & 1 else bit) * (1 << b)
        return total

    def dp_peer(b):
        bit = (dp // (1 << b)) % 2
        return dp + (1 - 2 * bit) * (1 << b)

    loads = [(x_in, x), (ur_in.at[0], ur.at[0]), (g_in, g), (dl_in.at[0], dl.at[0])]
    for q in range(1, groups):
        loads += [(ur_in.at[q], ur.at[q]), (dl_in.at[q], dl.at[q])]
    loads += [(ul_in, ul), (df_in, df)]
    loads = [pltpu.make_async_copy(a, b, in_sem.at[i]) for i, (a, b) in enumerate(loads)]
    for c in loads:
        c.start()

    barrier = pltpu.get_barrier_semaphore()
    for k in range(1, mp_ways):
        pl.semaphore_signal(barrier, inc=1, device_id={"mp": mp_peer(k)}, device_id_type=MESH_IDS)
    for b in range(3):
        pl.semaphore_signal(barrier, inc=1, device_id={"dp": dp_peer(b)}, device_id_type=MESH_IDS)

    def pack(slot):
        piece = 16

        def one(s, carry):
            rows_in = pl.ds(pl.multiple_of(s * piece * blocks, piece * blocks), piece * blocks)
            for kind, scr in enumerate((scr0, scr1)):
                stage[slot, kind, pl.ds(s * piece, piece)] = scr[rows_in, :].reshape(piece, blocks, tok).astype(BF16)
            return carry

        lax.fori_loop(0, width // piece, one, 0)

    def send_chunk(slot, ch):
        n = slot * chunks + ch
        there = (slot, slice(None), pl.ds(ch * CHUNK, CHUNK), pl.ds(me * blocks, blocks))
        for k in list(range(2, mp_ways)) + [1]:
            p = mp_peer(k)
            pltpu.make_async_remote_copy(
                src_ref=stage.at[slot, :, pl.ds(p * blocks + ch * CHUNK, CHUNK)],
                dst_ref=land.at[there],
                send_sem=send_sem.at[slot],
                recv_sem=recv_sem.at[n],
                device_id={"mp": p},
                device_id_type=MESH_IDS,
            ).start()
        pltpu.make_async_copy(
            stage.at[slot, :, pl.ds(me * blocks + ch * CHUNK, CHUNK)], land.at[there], recv_sem.at[n]
        ).start()

    def send_all(slot):
        def one(ch, carry):
            send_chunk(slot, ch)
            return carry

        lax.fori_loop(0, chunks, one, 0)

    def wait_chunk(slot, ch):
        ref = land.at[slot, :, pl.ds(ch * CHUNK, CHUNK)]
        pltpu.make_async_copy(ref, ref, recv_sem.at[slot * chunks + ch]).wait()

    def panels(q):
        def one(s, carry):
            for u in range(4):
                i = s * 4 + u
                cols = pl.ds(pl.multiple_of(i * width, width), width)
                scr0[pl.ds(i, width, stride=blocks), :] = mm(ur[q, i], x[:, cols], 0, 1)
                scr1[pl.ds(i, width, stride=blocks), :] = mm(dl[q, i], g[:, cols], 1, 1)
            return carry

        lax.fori_loop(0, blocks // 4, one, 0)
        pack(q)

    half = CHUNK // 2
    units = [(0, pl.ds(0, CHUNK), True), (1, pl.ds(0, half), True), (1, pl.ds(half, half), False)]

    def hop_copy(h, src, dst, n, bit):
        pltpu.make_async_remote_copy(
            src_ref=src,
            dst_ref=dst,
            send_sem=hop_send.at[h],
            recv_sem=hop_recv.at[h, n],
            device_id={"dp": dp_peer(bit)},
            device_id_type=MESH_IDS,
        ).start()

    def hop1(n):
        for kind, bl, y_first in units:
            if y_first:
                src = part.at[n, kind, :, :, flip(yb), bl]
            else:
                src = part.at[n, kind, :, flip(zb), :, bl]
            hop_copy(0, src, got1.at[n, kind, :, :, bl], n, 0 if y_first else 1)

    def hop2(n):
        ref = got1.at[n]
        pltpu.make_async_copy(ref, ref, hop_recv.at[0, n]).wait()
        for kind, bl, y_first in units:
            at = (n, kind, slice(None), slice(None), yb, bl) if y_first else (n, kind, slice(None), zb, slice(None), bl)
            part[at] = (part[at].astype(F32) + got1[n, kind, :, :, bl].astype(F32)).astype(BF16)
        for kind, bl, y_first in units:
            src = part.at[n, kind, :, flip(zb), yb, bl] if y_first else part.at[n, kind, :, zb, flip(yb), bl]
            hop_copy(1, src, got2.at[n, kind, :, bl], n, 1 if y_first else 0)

    def hop3(n):
        ref = got2.at[n]
        pltpu.make_async_copy(ref, ref, hop_recv.at[1, n]).wait()
        for kind in range(2):
            at = (n, kind, slice(None), zb, yb)
            part[at] = (part[at].astype(F32) + got2[n, kind].astype(F32)).astype(BF16)
        for kind in range(2):
            hop_copy(2, part.at[n, kind, flip(wb), zb, yb], got3.at[n, kind], n, 2)

    def hop_end(n):
        ref = got3.at[n]
        pltpu.make_async_copy(ref, ref, hop_recv.at[2, n]).wait()
        for kind in range(2):
            total = part[n, kind, wb, zb, yb].astype(F32) + got3[n, kind].astype(F32)
            fin[n, kind] = total * scale
        q = (n // chunks) % groups
        at = (q, pl.ds((n % chunks) * CHUNK, CHUNK))

        @pl.when(n < mid_steps)
        def _():
            for kind, out in enumerate((gdf_out, gul_out)):
                pltpu.make_async_copy(fin.at[n, kind], out.at[at], out_sem.at[0]).start()

        @pl.when(n >= mid_steps)
        def _():
            for kind, out in enumerate((gdl_out, gur_out)):
                pltpu.make_async_copy(fin.at[n, kind], out.at[at], out_sem.at[0]).start()

    def hops(n):
        for lag, work in ((1, hop2), (2, hop3), (3, hop_end)):
            m = n - lag

            @pl.when((m >= 0) & (m < steps))
            def _():
                work(m)

    def keep(n, kind, b, value):
        part[n, kind, :, :, :, b] = value.astype(BF16).reshape(2, 2, 2, rows, width)

    def middle(n, q, c, b):
        w_ul, w_df = ul[q, c], df[q, c]
        cu, dg = land[q, 0, c], land[q, 1, c]
        pre = mm(w_ul, cu, 0, 0)
        sq = pre * pre
        th = jnp.tanh(gelu_root * (pre + gelu_cube * sq * pre))
        part1 = 0.5 * (1.0 + th)
        hidden = (pre * part1).astype(BF16)
        slope = part1 + 0.5 * pre * (1.0 - th * th) * (gelu_root * (1.0 + 3.0 * gelu_cube * sq))
        scr0[pl.ds(c, width, stride=blocks), :] = mm(w_df, hidden, 0, 0)
        pg = (mm(w_df, dg, 1, 0) * slope).astype(BF16)
        scr1[pl.ds(c, width, stride=blocks), :] = mm(w_ul, pg, 1, 0)
        keep(n, 0, b, mm(hidden, dg, 1, 1))
        keep(n, 1, b, mm(cu, pg, 1, 1))

    def mid_step(n, carry):
        q, ch = n // chunks, n % chunks
        wait_chunk(q, ch)

        def inner(s, c2):
            for u in range(UNROLL):
                b = s * UNROLL + u
                middle(n, q, ch * CHUNK + b, b)
            return c2

        lax.fori_loop(0, CHUNK // UNROLL, inner, 0)
        hop1(n)

        @pl.when(ch == chunks - 1)
        def _():
            pack(groups + q)
            send_all(groups + q)

        hops(n)
        return carry

    def last(n, q, e, b):
        cols = pl.ds(pl.multiple_of(e * width, width), width)
        cd, rg = land[groups + q, 0, e], land[groups + q, 1, e]
        keep(n, 0, b, mm(cd, g[:, cols], 1, 0))
        keep(n, 1, b, mm(rg, x[:, cols], 1, 0).T)
        one = mm(cd, dl[q, e], 0, 0)
        two = mm(ur[q, e], rg, 1, 0)
        if q > 0:
            one, two = one + acc_m[e], two + acc_t[e]
        if q < groups - 1:
            acc_m[e], acc_t[e] = one, two
        else:
            out_m[:, cols] = one.astype(BF16)
            out_t[:, cols] = two.T.astype(BF16)

    def last_step(q, ch):
        n = (groups + q) * chunks + ch
        wait_chunk(groups + q, ch)

        def inner(s, c2):
            for u in range(UNROLL):
                b = s * UNROLL + u
                last(n, q, ch * CHUNK + b, b)
            return c2

        lax.fori_loop(0, CHUNK // UNROLL, inner, 0)
        hop1(n)
        if q == groups - 1:
            cols = pl.ds(pl.multiple_of(ch * CHUNK * width, CHUNK * width), CHUNK * width)
            pltpu.make_async_copy(out_m.at[:, cols], mixed_out.at[:, cols], out_sem.at[1]).start()
            pltpu.make_async_copy(out_t.at[:, cols], tgrad_out.at[:, cols], out_sem.at[2]).start()
        hops(n)

    for c in loads[:4]:
        c.wait()
    panels(0)
    pl.semaphore_wait(barrier, mp_ways - 1 + 3)
    send_all(0)
    for q in range(1, groups):
        loads[2 + 2 * q].wait()
        loads[3 + 2 * q].wait()
        panels(q)
        send_all(q)
    loads[-2].wait()
    loads[-1].wait()
    lax.fori_loop(0, mid_steps, mid_step, 0)
    for q in range(groups):

        def one(ch, carry):
            last_step(q, ch)
            return carry

        lax.fori_loop(0, chunks, one, 0)

    def drain(n, carry):
        hops(n)
        return carry

    lax.fori_loop(steps, steps + 3, drain, 0)
    for slot in range(2 * groups):
        ref = stage.at[slot, :, pl.ds(0, (mp_ways - 1) * blocks)]
        pltpu.make_async_copy(ref, ref, send_sem.at[slot]).wait()
    for h, ref in enumerate((got1, got2, got3)):
        pltpu.make_async_copy(ref, ref, hop_send.at[h]).wait()
    pltpu.make_async_copy(fin, fin, out_sem.at[0]).wait()
    pltpu.make_async_copy(out_m, mixed_out, out_sem.at[1]).wait()
    pltpu.make_async_copy(out_t, tgrad_out, out_sem.at[2]).wait()


def fused(x, g, ur, ul, df, dl, mp_ways):
    groups, blocks, width = ur.shape[0], ur.shape[1], ur.shape[2]
    tok = x.shape[0]
    chunks = blocks // CHUNK
    steps = 2 * groups * chunks
    rows = width // 8
    act = jax.ShapeDtypeStruct(x.shape, BF16)
    grad = jax.ShapeDtypeStruct((groups, blocks, rows, width), F32)
    vm = pltpu.VMEM
    dma = pltpu.SemaphoreType.DMA
    return pl.pallas_call(
        functools.partial(fused_kernel, mp_ways),
        out_shape=[act] * 2 + [grad] * 4,
        in_specs=[pl.BlockSpec(memory_space=pl.ANY)] * 6,
        out_specs=[pl.BlockSpec(memory_space=pl.ANY)] * 6,
        scratch_shapes=[
            vm(x.shape, BF16),
            vm(x.shape, BF16),
            vm(ur.shape, BF16),
            vm(ur.shape, BF16),
            vm(ur.shape, BF16),
            vm(ur.shape, BF16),
            vm((width * blocks, tok), F32),
            vm((width * blocks, tok), F32),
            vm((2 * groups, 2, width, blocks, tok), BF16),
            vm((2 * groups, 2, blocks, width, tok), BF16),
            vm((steps, 2, 2, 2, 2, CHUNK, rows, width), BF16),
            vm((steps, 2, 2, 2, CHUNK, rows, width), BF16),
            vm((steps, 2, 2, CHUNK, rows, width), BF16),
            vm((steps, 2, CHUNK, rows, width), BF16),
            vm((steps, 2, CHUNK, rows, width), F32),
            vm((blocks, tok, width), F32),
            vm((blocks, width, tok), F32),
            vm(x.shape, BF16),
            vm(x.shape, BF16),
            dma((2 * groups + 4,)),
            dma((2 * groups,)),
            dma((steps,)),
            dma((3,)),
            dma((3, steps)),
            dma((3,)),
        ],
        compiler_params=pltpu.CompilerParams(
            vmem_limit_bytes=60 * 2**20, collective_id=0, has_side_effects=True
        ),
        cost_estimate=pl.CostEstimate(
            flops=48 * groups * blocks * width * width * tok // 2, bytes_accessed=14 * 2**20, transcendentals=0
        ),
    )(x, g, ur, ul, df, dl)


def body(tokens, cotangent, up_right, up_left, down_first_factor, down_left):
    groups, width = up_right.shape[0], up_right.shape[2]
    mp_ways, dp_ways = lax.axis_size("mp"), lax.axis_size("dp")
    if dp_ways == 8 and up_right.shape[1] % 16 == 0:
        return tuple(fused(tokens, cotangent, up_right, up_left, down_first_factor, down_left, mp_ways))
    scale = (dp_ways * tokens.shape[0]) ** (-0.5)
    me = jnp.stack([lax.axis_index("mp"), lax.axis_index("dp")]).astype(jnp.int32)
    firsts, seconds, reductions = [], [], []
    for q in range(groups):
        firsts.append(exchange(make_panels(me, tokens, cotangent, up_right, down_left, q, mp_ways)))
    for q in range(groups):
        panels, halves = make_middle(me, firsts[q], up_left, down_first_factor, q, dp_ways)
        seconds.append(exchange(panels))
        reductions.append(halves)
    for q in range(groups):
        reductions.append(make_last_grads(me, seconds[q], tokens, cotangent, width, dp_ways))
    sums = halving_rounds(reductions, scale)
    mid_sums, last_sums = sums[:groups], sums[groups:]
    mixed, tokens_grad = make_outputs(me, seconds, down_left, up_right)

    def pick(sums, kind):
        return jnp.stack([s[kind] for s in sums])

    return (mixed, tokens_grad, pick(last_sums, 1), pick(mid_sums, 1), pick(mid_sums, 0), pick(last_sums, 0))


def solution(mesh):
    weight = P(None, "mp", None, None)
    in_specs = (P("dp", "mp"), P("dp", "mp"), weight, weight, weight, weight)
    grad = P(None, "mp", "dp", None)
    out_specs = (P("dp", "mp"), P("dp", "mp"), grad, grad, grad, grad)
    return jax.shard_map(body, mesh=mesh, in_specs=in_specs, out_specs=out_specs, check_vma=False)
```

```python
import functools

import jax
import jax.numpy as jnp
from jax import lax
from jax.experimental import pallas as pl
from jax.experimental.pallas import tpu as pltpu
from jax.sharding import PartitionSpec as P

gelu_root = 0.7978845608
gelu_cube = 0.044715
F32 = jnp.float32
BF16 = jnp.bfloat16


def mm(lhs, rhs, ldim, rdim):
    return lax.dot_general(lhs, rhs, (((ldim,), (rdim,)), ((), ())), preferred_element_type=F32)


def send_panel(outs, kind, scratch, me, blocks):
    span = blocks * blocks
    for k, out in enumerate(outs):
        start = pl.multiple_of((me ^ k) * span, span)
        rows = scratch[pl.ds(start, span), :]
        out[kind] = rows.reshape(out.shape[1:]).astype(BF16)


def gather_rows(parts, kind, scratch, slot, me, block, blocks):
    for k, part in enumerate(parts):
        start = pl.multiple_of((me ^ k) * blocks, blocks)
        scratch[slot, pl.ds(start, blocks), :] = part[kind, block].astype(F32)
    return scratch[slot].astype(BF16)


def hop_order(ways, kind):
    bits = [1 << b for b in range(ways.bit_length() - 1)]
    return [bits[1], bits[0]] + bits[2:] if kind and len(bits) > 1 else bits


def store_grad(outs, kind, block, value, scratch, slot, me, ways):
    rows = value.shape[0] // ways
    first, *later = hop_order(ways, kind)
    scratch[slot] = value
    for p in range(ways // 2):
        rel = sum(bit for t, bit in enumerate(later) if p >> t & 1)
        for out, target in ((outs[2 * kind], rel), (outs[2 * kind + 1], rel + first)):
            start = pl.multiple_of((me ^ target) * rows, rows)
            out[p, block] = scratch[slot, pl.ds(start, rows), :].astype(BF16)


def panels_kernel(ways, me_ref, x_ref, g_ref, ur_ref, dl_ref, *rest):
    outs, scr_r, scr_b = rest[:ways], rest[ways], rest[ways + 1]
    blocks, width = ur_ref.shape[1], ur_ref.shape[2]
    me = me_ref[0]
    for i in range(blocks):
        cols = slice(i * width, (i + 1) * width)
        scr_r[pl.ds(i, width, stride=blocks), :] = mm(ur_ref[0, i], x_ref[:, cols], 0, 1)
        scr_b[pl.ds(i, width, stride=blocks), :] = mm(dl_ref[0, i], g_ref[:, cols], 1, 1)
    send_panel(outs, 0, scr_r, me, blocks)
    send_panel(outs, 1, scr_b, me, blocks)


def full_spec(shape):
    return pl.BlockSpec(shape, lambda s: (0,) * len(shape))


def group_spec(w, q):
    return pl.BlockSpec((1,) + w.shape[1:], lambda s: (q, 0, 0, 0))


def limits(flops, mib):
    return dict(
        compiler_params=pltpu.CompilerParams(vmem_limit_bytes=40 * 2**20),
        cost_estimate=pl.CostEstimate(flops=flops * 8, bytes_accessed=mib * 2**20, transcendentals=0),
    )


def make_panels(me, x, g, ur, dl, q, ways):
    tok, blocks, width = x.shape[0], ur.shape[1], ur.shape[2]
    part = jax.ShapeDtypeStruct((2, blocks, blocks, tok), BF16)
    return pl.pallas_call(
        functools.partial(panels_kernel, ways),
        out_shape=[part] * ways,
        grid=(1,),
        in_specs=[
            pl.BlockSpec(memory_space=pltpu.SMEM),
            full_spec(x.shape),
            full_spec(g.shape),
            group_spec(ur, q),
            group_spec(dl, q),
        ],
        out_specs=[full_spec(part.shape)] * ways,
        scratch_shapes=[pltpu.VMEM((width * blocks, tok), F32)] * 2,
        **limits(4 * tok * blocks * width * width, 8),
    )(me, x, g, ur, dl)


UNROLL = 4


def middle_kernel(mp_ways, dp_ways, me_ref, ul_ref, df_ref, *rest):
    n = mp_ways
    first_in, outs, grads = rest[:n], rest[n : 2 * n], rest[2 * n : 2 * n + 4]
    scr_d, scr_u, asm_r, asm_b, gr1, gr2 = rest[2 * n + 4 :]
    blocks, width = ul_ref.shape[1], ul_ref.shape[2]
    me_mp, me_dp = me_ref[0], me_ref[1]

    def one(c, slot):
        ul, df = ul_ref[0, c], df_ref[0, c]
        cu = gather_rows(first_in, 0, asm_r, slot, me_mp, c, blocks)
        dg = gather_rows(first_in, 1, asm_b, slot, me_mp, c, blocks)
        pre = mm(ul, cu, 0, 0)
        sq = pre * pre
        th = jnp.tanh(gelu_root * (pre + gelu_cube * sq * pre))
        half = 0.5 * (1.0 + th)
        hidden = (pre * half).astype(BF16)
        slope = half + 0.5 * pre * (1.0 - th * th) * (gelu_root * (1.0 + 3.0 * gelu_cube * sq))
        scr_d[pl.ds(c, width, stride=blocks), :] = mm(df, hidden, 0, 0)
        pg = (mm(df, dg, 1, 0) * slope).astype(BF16)
        scr_u[pl.ds(c, width, stride=blocks), :] = mm(ul, pg, 1, 0)
        store_grad(grads, 0, c, mm(hidden, dg, 1, 1), gr1, slot, me_dp, dp_ways)
        store_grad(grads, 1, c, mm(cu, pg, 1, 1), gr2, slot, me_dp, dp_ways)

    def step(s, carry):
        for slot in range(UNROLL):
            one(s * UNROLL + slot, slot)
        return carry

    lax.fori_loop(0, blocks // UNROLL, step, 0)
    send_panel(outs, 0, scr_d, me_mp, blocks)
    send_panel(outs, 1, scr_u, me_mp, blocks)


def grad_halves(blocks, width, dp_ways):
    return jax.ShapeDtypeStruct((dp_ways // 2, blocks, width // dp_ways, width), BF16)


def make_middle(me, first_in, ul, df, q, dp_ways):
    n = len(first_in)
    part = jax.ShapeDtypeStruct(first_in[0].shape, BF16)
    blocks, width, tok = ul.shape[1], ul.shape[2], part.shape[3]
    half = grad_halves(blocks, width, dp_ways)
    res = pl.pallas_call(
        functools.partial(middle_kernel, n, dp_ways),
        out_shape=[part] * n + [half] * 4,
        grid=(1,),
        in_specs=[pl.BlockSpec(memory_space=pltpu.SMEM)] + [group_spec(ul, q)] * 2 + [full_spec(part.shape)] * n,
        out_specs=[full_spec(part.shape)] * n + [full_spec(half.shape)] * 4,
        scratch_shapes=[pltpu.VMEM((width * blocks, tok), F32)] * 2
        + [pltpu.VMEM((UNROLL, width, tok), F32)] * 2
        + [pltpu.VMEM((UNROLL, width, width), F32)] * 2,
        **limits(12 * tok * blocks * width * width, 8),
    )(me, ul, df, *first_in)
    return res[:n], res[n:]


def last_grads_kernel(mp_ways, dp_ways, me_ref, x_ref, g_ref, *rest):
    n = mp_ways
    second_in, grads = rest[:n], rest[n : n + 4]
    asm_d, asm_u, gr1, gr2 = rest[n + 4 :]
    blocks = second_in[0].shape[1]
    width = gr1.shape[1]
    me_mp, me_dp = me_ref[0], me_ref[1]
    for e in range(blocks):
        cols = slice(e * width, (e + 1) * width)
        slot = e % UNROLL
        cd = gather_rows(second_in, 0, asm_d, slot, me_mp, e, blocks)
        rg = gather_rows(second_in, 1, asm_u, slot, me_mp, e, blocks)
        store_grad(grads, 0, e, mm(cd, g_ref[:, cols], 1, 0), gr1, slot, me_dp, dp_ways)
        store_grad(grads, 1, e, mm(rg, x_ref[:, cols], 1, 0).T, gr2, slot, me_dp, dp_ways)


def make_last_grads(me, second_in, x, g, width, dp_ways):
    n = len(second_in)
    part = second_in[0]
    blocks, tok = part.shape[1], part.shape[3]
    half = grad_halves(blocks, width, dp_ways)
    return pl.pallas_call(
        functools.partial(last_grads_kernel, n, dp_ways),
        out_shape=[half] * 4,
        grid=(1,),
        in_specs=[pl.BlockSpec(memory_space=pltpu.SMEM)] + [full_spec(x.shape)] * 2 + [full_spec(part.shape)] * n,
        out_specs=[full_spec(half.shape)] * 4,
        scratch_shapes=[pltpu.VMEM((UNROLL, width, tok), F32)] * 2 + [pltpu.VMEM((UNROLL, width, width), F32)] * 2,
        **limits(4 * tok * blocks * width * width, 6),
    )(me, x, g, *second_in)


def outputs_kernel(mp_ways, me_ref, dl_ref, ur_ref, *rest):
    n = mp_ways
    groups = dl_ref.shape[0]
    second_in = rest[: groups * n]
    mixed, tgrad, asm_d, asm_u = rest[groups * n :]
    blocks, width = dl_ref.shape[1], dl_ref.shape[2]
    me_mp = me_ref[0]
    for e in range(blocks):
        cols = slice(e * width, (e + 1) * width)
        out_sum = grad_sum = None
        for q in range(groups):
            parts = second_in[q * n : (q + 1) * n]
            slot = (e * groups + q) % UNROLL
            cd = gather_rows(parts, 0, asm_d, slot, me_mp, e, blocks)
            rg = gather_rows(parts, 1, asm_u, slot, me_mp, e, blocks)
            one = mm(cd, dl_ref[q, e], 0, 0)
            two = mm(ur_ref[q, e], rg, 1, 0)
            out_sum = one if q == 0 else out_sum + one
            grad_sum = two if q == 0 else grad_sum + two
        mixed[:, cols] = out_sum.astype(BF16)
        tgrad[:, cols] = grad_sum.T.astype(BF16)


def make_outputs(me, second_in, dl, ur):
    n = len(second_in[0])
    part = second_in[0][0]
    groups, blocks, width, tok = dl.shape[0], dl.shape[1], dl.shape[2], part.shape[3]
    out = jax.ShapeDtypeStruct((tok, blocks * width), BF16)
    return pl.pallas_call(
        functools.partial(outputs_kernel, n),
        out_shape=[out] * 2,
        grid=(1,),
        in_specs=[pl.BlockSpec(memory_space=pltpu.SMEM)]
        + [full_spec(dl.shape)] * 2
        + [full_spec(part.shape)] * (n * groups),
        out_specs=[full_spec(out.shape)] * 2,
        scratch_shapes=[pltpu.VMEM((UNROLL, width, tok), F32)] * 2,
        **limits(8 * tok * blocks * width * width, 10),
    )(me, dl, ur, *[p for parts in second_in for p in parts])


def xor_permute(array, axis, k):
    return lax.ppermute(array, axis, [(i, i ^ k) for i in range(lax.axis_size(axis))])


def exchange(parts):
    return [p if k == 0 else xor_permute(p, "mp", k) for k, p in enumerate(parts)]


def halving_rounds(reductions, scale):
    ways = lax.axis_size("dp")
    orders = [hop_order(ways, kind) for kind in range(2)]
    hops = len(orders[0])
    pairs = [[[h[0], h[1]], [h[2], h[3]]] for h in reductions]
    sums = [[None, None] for _ in reductions]
    for turn in range(hops + len(reductions) - 1):
        active = [(s, kind) for s in range(len(reductions)) if 0 <= turn - s < hops for kind in range(2)]
        got = [xor_permute(pairs[s][kind][1], "dp", orders[kind][turn - s]) for s, kind in active]
        got = lax.optimization_barrier(got)
        for (s, kind), arrived in zip(active, got):
            total = pairs[s][kind][0].astype(F32) + arrived.astype(F32)
            if total.shape[0] == 1:
                sums[s][kind] = total[0] * scale
                continue
            total = total.astype(BF16).reshape((total.shape[0] // 2, 2) + total.shape[1:])
            pairs[s][kind] = [total[:, 0], total[:, 1]]
    return sums


MSG = 8
CHUNK = 4
FINE = 2
FINES = 4
LAGS = (2, 4, 6)
MESH_IDS = pl.DeviceIdType.MESH
HBM = pl.BlockSpec(memory_space=pltpu.HBM)
VMEM = pl.BlockSpec(memory_space=pltpu.VMEM)


def flip(v):
    return 1 - v


def fused_kernel(
    mp_ways,
    x_in,
    g_in,
    ur_in,
    ul_in,
    df_in,
    dl_in,
    mixed,
    tgrad,
    gur,
    gul,
    gdf,
    gdl,
    x,
    g,
    ur,
    ul,
    df,
    dl,
    scr0,
    scr1,
    stage,
    land,
    part,
    got1,
    got2,
    got3,
    fpart,
    fgot1,
    fgot2,
    in_sem,
    send_sem,
    recv_sem,
    frecv_sem,
    hop_send,
    hop_recv,
    fhop_send,
    fhop_recv,
):
    groups, blocks, width = ur.shape[0], ur.shape[1], ur.shape[2]
    tok = x.shape[0]
    chunks, msgs, ratio = blocks // CHUNK, blocks // MSG, MSG // CHUNK
    fine_first = blocks - FINES * FINE
    rows = width // 8
    half_width = width // 2
    fine_slot = 2 * groups - 1
    steps = fine_slot * chunks + fine_first // CHUNK
    mid_steps = groups * chunks
    scale = (8 * tok) ** (-0.5)
    me, dp = lax.axis_index("mp"), lax.axis_index("dp")
    yb, zb, wb = dp % 2, (dp // 2) % 2, dp // 4
    top = mp_ways // 2
    other = flip(me // top)

    def mp_peer(k):
        total = 0
        for b in range(mp_ways.bit_length() - 1):
            bit = (me // (1 << b)) % 2
            total = total + (flip(bit) if k >> b & 1 else bit) * (1 << b)
        return total

    def dp_peer(mask):
        peer = dp
        for b in range(3):
            if mask >> b & 1:
                peer = peer + (1 - 2 * ((dp // (1 << b)) % 2)) * (1 << b)
        return peer

    def mp_id(k):
        return dict(device_id={"mp": mp_peer(k)}, device_id_type=MESH_IDS)

    def dp_id(mask):
        return dict(device_id={"dp": dp_peer(mask)}, device_id_type=MESH_IDS)

    loads = [(x_in, x), (ur_in.at[0], ur.at[0]), (g_in, g), (dl_in.at[0], dl.at[0])]
    for q in range(1, groups):
        loads += [(ur_in.at[q], ur.at[q]), (dl_in.at[q], dl.at[q])]
    loads += [(ul_in, ul), (df_in, df)]
    loads = [pltpu.make_async_copy(a, b, in_sem.at[i]) for i, (a, b) in enumerate(loads)]
    for c in loads:
        c.start()

    barrier = pltpu.get_barrier_semaphore()
    dp_masks = (1, 2, 4, 6)
    for k in range(1, mp_ways):
        pl.semaphore_signal(barrier, inc=1, **mp_id(k))
    for mask in dp_masks:
        pl.semaphore_signal(barrier, inc=1, **dp_id(mask))

    piece = 16

    def pack(slot, kind, first, count):
        scr = (scr0, scr1)[kind]

        def one(s, carry):
            c = first + s * piece
            rows_in = pl.ds(pl.multiple_of(c * blocks, piece * blocks), piece * blocks)
            stage[slot % groups, kind, pl.ds(c, piece)] = scr[rows_in, :].reshape(piece, blocks, tok).astype(BF16)
            return carry

        lax.fori_loop(0, count // piece, one, 0)

    def send(slot, first, size, sems, ks):
        there = (slot, slice(None), pl.ds(first, size), pl.ds(me * blocks, blocks))
        for k in ks:
            src = stage.at[slot % groups, :, pl.ds(mp_peer(k) * blocks + first, size)]
            if k:
                pltpu.make_async_remote_copy(
                    src_ref=src, dst_ref=land.at[there], send_sem=send_sem.at[slot], recv_sem=sems, **mp_id(k)
                ).start()
            else:
                pltpu.make_async_copy(src, land.at[there], sems).start()

    far, near = range(top, mp_ways), range(top)

    def send_all(slot, ks):
        size = CHUNK if slot == fine_slot else MSG

        def coarse(m):
            send(slot, m * size, size, recv_sem.at[slot * msgs + m], ks)

        loop(0, fine_first // CHUNK if slot == fine_slot else msgs, coarse)
        if slot == fine_slot:
            for f in range(FINES):
                send(slot, fine_first + f * FINE, FINE, frecv_sem.at[f], ks)

    def sent(slot):
        arrived(stage.at[slot % groups, :, pl.ds(0, (mp_ways - 1) * blocks)], send_sem.at[slot])

    def wait_msg(slot, ch):
        if slot == fine_slot:
            arrived(land.at[slot, :, pl.ds(ch * CHUNK, CHUNK)], recv_sem.at[slot * msgs + ch])
            return

        @pl.when(ch % ratio == 0)
        def _():
            arrived(land.at[slot, :, pl.ds(ch * CHUNK, MSG)], recv_sem.at[slot * msgs + ch // ratio])

    def panel(q, kind, part_of):
        first = part_of * half_width
        cs = slice(first, first + half_width)

        def one(s, carry):
            for u in range(4):
                i = s * 4 + u
                cols = pl.ds(pl.multiple_of(i * width, width), width)
                to = pl.ds(first * blocks + i, half_width, stride=blocks)
                if kind == 0:
                    scr0[to, :] = mm(ur[q, i, :, cs], x[:, cols], 0, 1)
                else:
                    scr1[to, :] = mm(dl[q, i, cs, :], g[:, cols], 1, 1)
            return carry

        lax.fori_loop(0, blocks // 4, one, 0)
        pack(q, kind, first, half_width)

    half = CHUNK // 2
    units = [(0, pl.ds(0, CHUNK), True), (1, pl.ds(0, half), True), (1, pl.ds(half, half), False)]

    def hop_copy(h, src, dst, n, mask):
        pltpu.make_async_remote_copy(
            src_ref=src, dst_ref=dst, send_sem=hop_send.at[h], recv_sem=hop_recv.at[h, n], **dp_id(mask)
        ).start()

    def arrived(ref, sem):
        pltpu.make_async_copy(ref, ref, sem).wait()

    def add_into(ref, at, value):
        ref[at] = (ref[at].astype(F32) + value.astype(F32)).astype(BF16)

    def hop1(n):
        for kind, bl, y_first in units:
            if y_first:
                src = part.at[n, kind, :, :, flip(yb), bl]
            else:
                src = part.at[n, kind, :, flip(zb), :, bl]
            hop_copy(0, src, got1.at[n, kind, :, :, bl], n, 1 if y_first else 2)

    every = slice(None)

    def hop2(n):
        arrived(got1.at[n], hop_recv.at[0, n])
        for kind, bl, y_first in units:
            at = (n, kind, every, every, yb, bl) if y_first else (n, kind, every, zb, every, bl)
            add_into(part, at, got1[n, kind, :, :, bl])
        for kind, bl, y_first in units:
            src = part.at[n, kind, :, flip(zb), yb, bl] if y_first else part.at[n, kind, :, zb, flip(yb), bl]
            hop_copy(1, src, got2.at[n, kind, :, bl], n, 2 if y_first else 1)

    def hop3(n):
        arrived(got2.at[n], hop_recv.at[1, n])
        for kind in range(2):
            add_into(part, (n, kind, every, zb, yb), got2[n, kind])
        for kind in range(2):
            hop_copy(2, part.at[n, kind, flip(wb), zb, yb], got3.at[n, kind], n, 4)

    def hop_end(n):
        arrived(got3.at[n], hop_recv.at[2, n])
        sums = [(part[n, k, wb, zb, yb].astype(F32) + got3[n, k].astype(F32)) * scale for k in range(2)]
        at = ((n // chunks) % groups, pl.ds((n % chunks) * CHUNK, CHUNK))

        def to_mid():
            gdf[at], gul[at] = sums

        def to_last():
            gdl[at], gur[at] = sums

        if isinstance(n, int):
            (to_mid if n < mid_steps else to_last)()
        else:
            pl.when(n < mid_steps)(to_mid)
            pl.when(n >= mid_steps)(to_last)

    def hops(n):
        for lag, work in zip(LAGS, (hop2, hop3, hop_end)):
            m = n - lag

            @pl.when((m >= 0) & (m < steps))
            def _():
                work(m)

    def fine1(f):
        for kind in range(2):
            pltpu.make_async_remote_copy(
                src_ref=fpart.at[f, kind, :, :, flip(yb)],
                dst_ref=fgot1.at[f, kind],
                send_sem=fhop_send.at[0],
                recv_sem=fhop_recv.at[0, f],
                **dp_id(1),
            ).start()

    def fine2(f):
        arrived(fgot1.at[f], fhop_recv.at[0, f])
        for kind in range(2):
            add_into(fpart, (f, kind, every, every, yb), fgot1[f, kind])
        for r in (3, 2, 1):
            to_w, to_z = flip(wb) if r >> 1 else wb, flip(zb) if r & 1 else zb
            pltpu.make_async_remote_copy(
                src_ref=fpart.at[f, :, to_w, to_z, yb],
                dst_ref=fgot2.at[f, r - 1],
                send_sem=fhop_send.at[1],
                recv_sem=fhop_recv.at[1, f],
                **dp_id(2 * r),
            ).start()

    def fine_out(f, totals):
        at = (groups - 1, pl.ds(fine_first + f * FINE, FINE))
        for total, out in zip(totals, (gdl, gur)):
            out[at] = total * scale

    def fine_end(f):
        arrived(fgot2.at[f], fhop_recv.at[1, f])
        totals = []
        for kind in range(2):
            total = fpart[f, kind, wb, zb, yb].astype(F32)
            for r in range(3):
                total = total + fgot2[f, r, kind].astype(F32)
            totals.append(total)
        fine_out(f, totals)

    def keep(dst, n, kind, b, value):
        dst[n, kind, :, :, :, b] = value.astype(BF16).reshape(2, 2, 2, rows, width)

    def middle(n, q, c, b):
        w_ul, w_df = ul[q, c], df[q, c]
        cu, dg = land[q, 0, c], land[q, 1, c]
        pre = mm(w_ul, cu, 0, 0)
        sq = pre * pre
        th = jnp.tanh(gelu_root * (pre + gelu_cube * sq * pre))
        part1 = 0.5 * (1.0 + th)
        hidden = (pre * part1).astype(BF16)
        slope = part1 + 0.5 * pre * (1.0 - th * th) * (gelu_root * (1.0 + 3.0 * gelu_cube * sq))
        scr0[pl.ds(c, width, stride=blocks), :] = mm(w_df, hidden, 0, 0)
        pg = (mm(w_df, dg, 1, 0) * slope).astype(BF16)
        scr1[pl.ds(c, width, stride=blocks), :] = mm(w_ul, pg, 1, 0)
        keep(part, n, 0, b, mm(hidden, dg, 1, 1))
        keep(part, n, 1, b, mm(cu, pg, 1, 1))

    def mid_step(q, ch):
        n = q * chunks + ch
        wait_msg(q, ch)
        for b in range(CHUNK):
            middle(n, q, ch * CHUNK + b, b)
        hop1(n)
        hops(n)

    def columns(e):
        return pl.ds(pl.multiple_of(e * width, width), width)

    def last_grads(dst, n, q, e, b):
        cd, rg = land[groups + q, 0, e], land[groups + q, 1, e]
        keep(dst, n, 0, b, mm(cd, g[:, columns(e)], 1, 0))
        keep(dst, n, 1, b, mm(rg, x[:, columns(e)], 1, 0).T)

    def last_outs(q, e):
        cd, rg = land[groups + q, 0, e], land[groups + q, 1, e]
        one = mm(cd, dl[q, e], 0, 0)
        two = mm(ur[q, e], rg, 1, 0)
        if q > 0:
            one, two = one + scr0[columns(e), :], two + scr1[columns(e), :]
        if q < groups - 1:
            scr0[columns(e), :], scr1[columns(e), :] = one, two
        else:
            mixed[:, columns(e)] = one.astype(BF16)
            tgrad[:, columns(e)] = two.T.astype(BF16)

    def last_step(q, ch):
        n = (groups + q) * chunks + ch
        wait_msg(groups + q, ch)
        for b in range(CHUNK):
            last_grads(part, n, q, ch * CHUNK + b, b)
            last_outs(q, ch * CHUNK + b)
        hop1(n)
        hops(n)

    def fine_step(f):
        q = groups - 1
        first = fine_first + f * FINE
        arrived(land.at[fine_slot, :, pl.ds(first, FINE)], frecv_sem.at[f])
        for b in range(FINE):
            last_grads(fpart, f, q, first + b, b)
        fine1(f)
        for b in range(FINE):
            last_outs(q, first + b)

    def loop(start, end, work):
        def one(i, carry):
            work(i)
            return carry

        lax.fori_loop(start, end, one, 0)

    for kind in range(2):
        loads[2 * kind].wait()
        loads[2 * kind + 1].wait()
        for h in range(2):
            pl.when(other == h)(functools.partial(panel, 0, kind, h))
    pl.semaphore_wait(barrier, mp_ways - 1 + len(dp_masks))
    send_all(0, far)
    for kind in range(2):
        for h in range(2):
            pl.when(other != h)(functools.partial(panel, 0, kind, h))
    send_all(0, near)
    for q in range(1, groups):
        for kind in range(2):
            loads[2 + 2 * q + kind].wait()
            for h in range(2):
                panel(q, kind, h)
        send_all(q, [*far, *near])
    loads[-2].wait()
    loads[-1].wait()
    for q in range(groups):
        loop(0, chunks, functools.partial(mid_step, q))
        sent(q)
        for kind in range(2):
            pack(groups + q, kind, 0, width)
        send_all(groups + q, [*far, *near])
    for q in range(groups):
        loop(0, chunks if q < groups - 1 else fine_first // CHUNK, functools.partial(last_step, q))
    fine_step(0)
    hop2(steps - 2)
    hop3(steps - 4)
    hop_end(steps - 6)
    fine_step(1)
    fine_step(2)
    hop2(steps - 1)
    hop3(steps - 3)
    hop_end(steps - 5)
    fine_step(3)
    fine2(0)
    hop3(steps - 2)
    fine2(1)
    hop_end(steps - 4)
    fine2(2)
    hop3(steps - 1)
    fine2(3)
    hop_end(steps - 3)
    fine_end(0)
    hop_end(steps - 2)
    fine_end(1)
    fine_end(2)
    hop_end(steps - 1)
    fine_end(3)
    for q in range(groups):
        sent(groups + q)
    for h, ref in enumerate((got1, got2, got3)):
        arrived(ref, hop_send.at[h])
    for h, ref in enumerate((fgot1, fgot2)):
        arrived(ref, fhop_send.at[h])


def finish_kernel(*refs):
    n = (len(refs) - 1) // 2
    copies = [pltpu.make_async_copy(refs[i], refs[n + i], refs[-1].at[i]) for i in range(n)]
    for c in copies:
        c.start()
    for c in copies:
        c.wait()


def finish(arrays):
    return pl.pallas_call(
        finish_kernel,
        out_shape=[jax.ShapeDtypeStruct(a.shape, a.dtype) for a in arrays],
        in_specs=[VMEM] * len(arrays),
        out_specs=[pl.BlockSpec(memory_space=pl.ANY)] * len(arrays),
        scratch_shapes=[pltpu.SemaphoreType.DMA((len(arrays),))],
        compiler_params=pltpu.CompilerParams(vmem_limit_bytes=16 * 2**20),
    )(*arrays)


def fused(x, g, ur, ul, df, dl, mp_ways):
    groups, blocks, width = ur.shape[0], ur.shape[1], ur.shape[2]
    tok = x.shape[0]
    steps = (2 * groups * blocks - FINES * FINE) // CHUNK
    rows = width // 8
    act = jax.ShapeDtypeStruct(x.shape, BF16)
    grad = jax.ShapeDtypeStruct((groups, blocks, rows, width), F32)
    vm = pltpu.VMEM
    dma = pltpu.SemaphoreType.DMA
    return pl.pallas_call(
        functools.partial(fused_kernel, mp_ways),
        out_shape=[act] * 2 + [grad] * 4,
        in_specs=[HBM] * 6,
        out_specs=[VMEM] * 6,
        scratch_shapes=[
            vm(x.shape, BF16),
            vm(x.shape, BF16),
            vm(ur.shape, BF16),
            vm(ur.shape, BF16),
            vm(ur.shape, BF16),
            vm(ur.shape, BF16),
            vm((width * blocks, tok), F32),
            vm((width * blocks, tok), F32),
            vm((groups, 2, width, blocks, tok), BF16),
            vm((2 * groups, 2, blocks, width, tok), BF16),
            vm((steps, 2, 2, 2, 2, CHUNK, rows, width), BF16),
            vm((steps, 2, 2, 2, CHUNK, rows, width), BF16),
            vm((steps, 2, 2, CHUNK, rows, width), BF16),
            vm((steps, 2, CHUNK, rows, width), BF16),
            vm((FINES, 2, 2, 2, 2, FINE, rows, width), BF16),
            vm((FINES, 2, 2, 2, FINE, rows, width), BF16),
            vm((FINES, 3, 2, FINE, rows, width), BF16),
            dma((2 * groups + 4,)),
            dma((2 * groups,)),
            dma((2 * groups * blocks // MSG + blocks // CHUNK,)),
            dma((FINES,)),
            dma((3,)),
            dma((3, steps)),
            dma((2,)),
            dma((2, FINES)),
        ],
        compiler_params=pltpu.CompilerParams(
            vmem_limit_bytes=48 * 2**20, collective_id=0, has_side_effects=True
        ),
        cost_estimate=pl.CostEstimate(
            flops=48 * groups * blocks * width * width * tok // 2, bytes_accessed=14 * 2**20, transcendentals=0
        ),
    )(x, g, ur, ul, df, dl)


def body(tokens, cotangent, up_right, up_left, down_first_factor, down_left):
    groups, width = up_right.shape[0], up_right.shape[2]
    mp_ways, dp_ways = lax.axis_size("mp"), lax.axis_size("dp")
    if dp_ways == 8 and up_right.shape[1] % 16 == 0:
        return tuple(finish(fused(tokens, cotangent, up_right, up_left, down_first_factor, down_left, mp_ways)))
    scale = (dp_ways * tokens.shape[0]) ** (-0.5)
    me = jnp.stack([lax.axis_index("mp"), lax.axis_index("dp")]).astype(jnp.int32)
    firsts, seconds, reductions = [], [], []
    for q in range(groups):
        firsts.append(exchange(make_panels(me, tokens, cotangent, up_right, down_left, q, mp_ways)))
    for q in range(groups):
        panels, halves = make_middle(me, firsts[q], up_left, down_first_factor, q, dp_ways)
        seconds.append(exchange(panels))
        reductions.append(halves)
    for q in range(groups):
        reductions.append(make_last_grads(me, seconds[q], tokens, cotangent, width, dp_ways))
    sums = halving_rounds(reductions, scale)
    mid_sums, last_sums = sums[:groups], sums[groups:]
    mixed, tokens_grad = make_outputs(me, seconds, down_left, up_right)

    def pick(sums, kind):
        return jnp.stack([s[kind] for s in sums])

    return (mixed, tokens_grad, pick(last_sums, 1), pick(mid_sums, 1), pick(mid_sums, 0), pick(last_sums, 0))


def solution(mesh):
    weight = P(None, "mp", None, None)
    in_specs = (P("dp", "mp"), P("dp", "mp"), weight, weight, weight, weight)
    grad = P(None, "mp", "dp", None)
    out_specs = (P("dp", "mp"), P("dp", "mp"), grad, grad, grad, grad)
    return jax.shard_map(body, mesh=mesh, in_specs=in_specs, out_specs=out_specs, check_vma=False)
```

```python
import functools

import jax
import jax.numpy as jnp
from jax import lax
from jax.experimental import pallas as pl
from jax.experimental.pallas import tpu as pltpu
from jax.sharding import PartitionSpec as P

gelu_root = 0.7978845608
gelu_cube = 0.044715
F32 = jnp.float32
BF16 = jnp.bfloat16


def mm(lhs, rhs, ldim, rdim):
    return lax.dot_general(lhs, rhs, (((ldim,), (rdim,)), ((), ())), preferred_element_type=F32)


def send_panel(outs, kind, scratch, me, blocks):
    span = blocks * blocks
    for k, out in enumerate(outs):
        start = pl.multiple_of((me ^ k) * span, span)
        rows = scratch[pl.ds(start, span), :]
        out[kind] = rows.reshape(out.shape[1:]).astype(BF16)


def gather_rows(parts, kind, scratch, slot, me, block, blocks):
    for k, part in enumerate(parts):
        start = pl.multiple_of((me ^ k) * blocks, blocks)
        scratch[slot, pl.ds(start, blocks), :] = part[kind, block].astype(F32)
    return scratch[slot].astype(BF16)


def hop_order(ways, kind):
    bits = [1 << b for b in range(ways.bit_length() - 1)]
    return [bits[1], bits[0]] + bits[2:] if kind and len(bits) > 1 else bits


def store_grad(outs, kind, block, value, scratch, slot, me, ways):
    rows = value.shape[0] // ways
    first, *later = hop_order(ways, kind)
    scratch[slot] = value
    for p in range(ways // 2):
        rel = sum(bit for t, bit in enumerate(later) if p >> t & 1)
        for out, target in ((outs[2 * kind], rel), (outs[2 * kind + 1], rel + first)):
            start = pl.multiple_of((me ^ target) * rows, rows)
            out[p, block] = scratch[slot, pl.ds(start, rows), :].astype(BF16)


def panels_kernel(ways, me_ref, x_ref, g_ref, ur_ref, dl_ref, *rest):
    outs, scr_r, scr_b = rest[:ways], rest[ways], rest[ways + 1]
    blocks, width = ur_ref.shape[1], ur_ref.shape[2]
    me = me_ref[0]
    for i in range(blocks):
        cols = slice(i * width, (i + 1) * width)
        scr_r[pl.ds(i, width, stride=blocks), :] = mm(ur_ref[0, i], x_ref[:, cols], 0, 1)
        scr_b[pl.ds(i, width, stride=blocks), :] = mm(dl_ref[0, i], g_ref[:, cols], 1, 1)
    send_panel(outs, 0, scr_r, me, blocks)
    send_panel(outs, 1, scr_b, me, blocks)


def full_spec(shape):
    return pl.BlockSpec(shape, lambda s: (0,) * len(shape))


def group_spec(w, q):
    return pl.BlockSpec((1,) + w.shape[1:], lambda s: (q, 0, 0, 0))


def limits(flops, mib):
    return dict(
        compiler_params=pltpu.CompilerParams(vmem_limit_bytes=40 * 2**20),
        cost_estimate=pl.CostEstimate(flops=flops * 8, bytes_accessed=mib * 2**20, transcendentals=0),
    )


def make_panels(me, x, g, ur, dl, q, ways):
    tok, blocks, width = x.shape[0], ur.shape[1], ur.shape[2]
    part = jax.ShapeDtypeStruct((2, blocks, blocks, tok), BF16)
    return pl.pallas_call(
        functools.partial(panels_kernel, ways),
        out_shape=[part] * ways,
        grid=(1,),
        in_specs=[
            pl.BlockSpec(memory_space=pltpu.SMEM),
            full_spec(x.shape),
            full_spec(g.shape),
            group_spec(ur, q),
            group_spec(dl, q),
        ],
        out_specs=[full_spec(part.shape)] * ways,
        scratch_shapes=[pltpu.VMEM((width * blocks, tok), F32)] * 2,
        **limits(4 * tok * blocks * width * width, 8),
    )(me, x, g, ur, dl)


UNROLL = 4


def middle_kernel(mp_ways, dp_ways, me_ref, ul_ref, df_ref, *rest):
    n = mp_ways
    first_in, outs, grads = rest[:n], rest[n : 2 * n], rest[2 * n : 2 * n + 4]
    scr_d, scr_u, asm_r, asm_b, gr1, gr2 = rest[2 * n + 4 :]
    blocks, width = ul_ref.shape[1], ul_ref.shape[2]
    me_mp, me_dp = me_ref[0], me_ref[1]

    def one(c, slot):
        ul, df = ul_ref[0, c], df_ref[0, c]
        cu = gather_rows(first_in, 0, asm_r, slot, me_mp, c, blocks)
        dg = gather_rows(first_in, 1, asm_b, slot, me_mp, c, blocks)
        pre = mm(ul, cu, 0, 0)
        sq = pre * pre
        th = jnp.tanh(gelu_root * (pre + gelu_cube * sq * pre))
        half = 0.5 * (1.0 + th)
        hidden = (pre * half).astype(BF16)
        slope = half + 0.5 * pre * (1.0 - th * th) * (gelu_root * (1.0 + 3.0 * gelu_cube * sq))
        scr_d[pl.ds(c, width, stride=blocks), :] = mm(df, hidden, 0, 0)
        pg = (mm(df, dg, 1, 0) * slope).astype(BF16)
        scr_u[pl.ds(c, width, stride=blocks), :] = mm(ul, pg, 1, 0)
        store_grad(grads, 0, c, mm(hidden, dg, 1, 1), gr1, slot, me_dp, dp_ways)
        store_grad(grads, 1, c, mm(cu, pg, 1, 1), gr2, slot, me_dp, dp_ways)

    def step(s, carry):
        for slot in range(UNROLL):
            one(s * UNROLL + slot, slot)
        return carry

    lax.fori_loop(0, blocks // UNROLL, step, 0)
    send_panel(outs, 0, scr_d, me_mp, blocks)
    send_panel(outs, 1, scr_u, me_mp, blocks)


def grad_halves(blocks, width, dp_ways):
    return jax.ShapeDtypeStruct((dp_ways // 2, blocks, width // dp_ways, width), BF16)


def make_middle(me, first_in, ul, df, q, dp_ways):
    n = len(first_in)
    part = jax.ShapeDtypeStruct(first_in[0].shape, BF16)
    blocks, width, tok = ul.shape[1], ul.shape[2], part.shape[3]
    half = grad_halves(blocks, width, dp_ways)
    res = pl.pallas_call(
        functools.partial(middle_kernel, n, dp_ways),
        out_shape=[part] * n + [half] * 4,
        grid=(1,),
        in_specs=[pl.BlockSpec(memory_space=pltpu.SMEM)] + [group_spec(ul, q)] * 2 + [full_spec(part.shape)] * n,
        out_specs=[full_spec(part.shape)] * n + [full_spec(half.shape)] * 4,
        scratch_shapes=[pltpu.VMEM((width * blocks, tok), F32)] * 2
        + [pltpu.VMEM((UNROLL, width, tok), F32)] * 2
        + [pltpu.VMEM((UNROLL, width, width), F32)] * 2,
        **limits(12 * tok * blocks * width * width, 8),
    )(me, ul, df, *first_in)
    return res[:n], res[n:]


def last_grads_kernel(mp_ways, dp_ways, me_ref, x_ref, g_ref, *rest):
    n = mp_ways
    second_in, grads = rest[:n], rest[n : n + 4]
    asm_d, asm_u, gr1, gr2 = rest[n + 4 :]
    blocks = second_in[0].shape[1]
    width = gr1.shape[1]
    me_mp, me_dp = me_ref[0], me_ref[1]
    for e in range(blocks):
        cols = slice(e * width, (e + 1) * width)
        slot = e % UNROLL
        cd = gather_rows(second_in, 0, asm_d, slot, me_mp, e, blocks)
        rg = gather_rows(second_in, 1, asm_u, slot, me_mp, e, blocks)
        store_grad(grads, 0, e, mm(cd, g_ref[:, cols], 1, 0), gr1, slot, me_dp, dp_ways)
        store_grad(grads, 1, e, mm(rg, x_ref[:, cols], 1, 0).T, gr2, slot, me_dp, dp_ways)


def make_last_grads(me, second_in, x, g, width, dp_ways):
    n = len(second_in)
    part = second_in[0]
    blocks, tok = part.shape[1], part.shape[3]
    half = grad_halves(blocks, width, dp_ways)
    return pl.pallas_call(
        functools.partial(last_grads_kernel, n, dp_ways),
        out_shape=[half] * 4,
        grid=(1,),
        in_specs=[pl.BlockSpec(memory_space=pltpu.SMEM)] + [full_spec(x.shape)] * 2 + [full_spec(part.shape)] * n,
        out_specs=[full_spec(half.shape)] * 4,
        scratch_shapes=[pltpu.VMEM((UNROLL, width, tok), F32)] * 2 + [pltpu.VMEM((UNROLL, width, width), F32)] * 2,
        **limits(4 * tok * blocks * width * width, 6),
    )(me, x, g, *second_in)


def outputs_kernel(mp_ways, me_ref, dl_ref, ur_ref, *rest):
    n = mp_ways
    groups = dl_ref.shape[0]
    second_in = rest[: groups * n]
    mixed, tgrad, asm_d, asm_u = rest[groups * n :]
    blocks, width = dl_ref.shape[1], dl_ref.shape[2]
    me_mp = me_ref[0]
    for e in range(blocks):
        cols = slice(e * width, (e + 1) * width)
        out_sum = grad_sum = None
        for q in range(groups):
            parts = second_in[q * n : (q + 1) * n]
            slot = (e * groups + q) % UNROLL
            cd = gather_rows(parts, 0, asm_d, slot, me_mp, e, blocks)
            rg = gather_rows(parts, 1, asm_u, slot, me_mp, e, blocks)
            one = mm(cd, dl_ref[q, e], 0, 0)
            two = mm(ur_ref[q, e], rg, 1, 0)
            out_sum = one if q == 0 else out_sum + one
            grad_sum = two if q == 0 else grad_sum + two
        mixed[:, cols] = out_sum.astype(BF16)
        tgrad[:, cols] = grad_sum.T.astype(BF16)


def make_outputs(me, second_in, dl, ur):
    n = len(second_in[0])
    part = second_in[0][0]
    groups, blocks, width, tok = dl.shape[0], dl.shape[1], dl.shape[2], part.shape[3]
    out = jax.ShapeDtypeStruct((tok, blocks * width), BF16)
    return pl.pallas_call(
        functools.partial(outputs_kernel, n),
        out_shape=[out] * 2,
        grid=(1,),
        in_specs=[pl.BlockSpec(memory_space=pltpu.SMEM)]
        + [full_spec(dl.shape)] * 2
        + [full_spec(part.shape)] * (n * groups),
        out_specs=[full_spec(out.shape)] * 2,
        scratch_shapes=[pltpu.VMEM((UNROLL, width, tok), F32)] * 2,
        **limits(8 * tok * blocks * width * width, 10),
    )(me, dl, ur, *[p for parts in second_in for p in parts])


def xor_permute(array, axis, k):
    return lax.ppermute(array, axis, [(i, i ^ k) for i in range(lax.axis_size(axis))])


def exchange(parts):
    return [p if k == 0 else xor_permute(p, "mp", k) for k, p in enumerate(parts)]


def halving_rounds(reductions, scale):
    ways = lax.axis_size("dp")
    orders = [hop_order(ways, kind) for kind in range(2)]
    hops = len(orders[0])
    pairs = [[[h[0], h[1]], [h[2], h[3]]] for h in reductions]
    sums = [[None, None] for _ in reductions]
    for turn in range(hops + len(reductions) - 1):
        active = [(s, kind) for s in range(len(reductions)) if 0 <= turn - s < hops for kind in range(2)]
        got = [xor_permute(pairs[s][kind][1], "dp", orders[kind][turn - s]) for s, kind in active]
        got = lax.optimization_barrier(got)
        for (s, kind), arrived in zip(active, got):
            total = pairs[s][kind][0].astype(F32) + arrived.astype(F32)
            if total.shape[0] == 1:
                sums[s][kind] = total[0] * scale
                continue
            total = total.astype(BF16).reshape((total.shape[0] // 2, 2) + total.shape[1:])
            pairs[s][kind] = [total[:, 0], total[:, 1]]
    return sums


MSG = 8
CHUNK = 4
FINE = 1
FINES = 4
LAGS = (2, 4, 6)
MESH_IDS = pl.DeviceIdType.MESH
HBM = pl.BlockSpec(memory_space=pltpu.HBM)
VMEM = pl.BlockSpec(memory_space=pltpu.VMEM)


def flip(v):
    return 1 - v


def fused_kernel(
    mp_ways,
    x_in,
    g_in,
    ur_in,
    ul_in,
    df_in,
    dl_in,
    mixed,
    tgrad,
    gur,
    gul,
    gdf,
    gdl,
    x,
    g,
    ur,
    ul,
    df,
    dl,
    scr0,
    scr1,
    stage,
    land,
    part,
    got1,
    got2,
    got3,
    fpart,
    fgot1,
    fgot2,
    in_sem,
    send_sem,
    recv_sem,
    frecv_sem,
    hop_send,
    hop_recv,
    fhop_send,
    fhop_recv,
):
    groups, blocks, width = ur.shape[0], ur.shape[1], ur.shape[2]
    tok = x.shape[0]
    chunks, msgs, ratio = blocks // CHUNK, blocks // MSG, MSG // CHUNK
    fine_first = blocks - FINES * FINE
    rows = width // 8
    half_width = width // 2
    fine_slot = 2 * groups - 1
    steps = fine_slot * chunks + fine_first // CHUNK
    mid_steps = groups * chunks
    scale = (8 * tok) ** (-0.5)
    me, dp = lax.axis_index("mp"), lax.axis_index("dp")
    yb, zb, wb = dp % 2, (dp // 2) % 2, dp // 4
    top = mp_ways // 2
    other = flip(me // top)

    def mp_peer(k):
        total = 0
        for b in range(mp_ways.bit_length() - 1):
            bit = (me // (1 << b)) % 2
            total = total + (flip(bit) if k >> b & 1 else bit) * (1 << b)
        return total

    def dp_peer(mask):
        peer = dp
        for b in range(3):
            if mask >> b & 1:
                peer = peer + (1 - 2 * ((dp // (1 << b)) % 2)) * (1 << b)
        return peer

    def mp_id(k):
        return dict(device_id={"mp": mp_peer(k)}, device_id_type=MESH_IDS)

    def dp_id(mask):
        return dict(device_id={"dp": dp_peer(mask)}, device_id_type=MESH_IDS)

    loads = [(x_in, x), (ur_in.at[0], ur.at[0]), (g_in, g), (dl_in.at[0], dl.at[0])]
    for q in range(1, groups):
        loads += [(ur_in.at[q], ur.at[q]), (dl_in.at[q], dl.at[q])]
    loads += [(ul_in, ul), (df_in, df)]
    loads = [pltpu.make_async_copy(a, b, in_sem.at[i]) for i, (a, b) in enumerate(loads)]
    for c in loads:
        c.start()

    barrier = pltpu.get_barrier_semaphore()
    dp_masks = (1, 2, 4, 6)
    for k in range(1, mp_ways):
        pl.semaphore_signal(barrier, inc=1, **mp_id(k))
    for mask in dp_masks:
        pl.semaphore_signal(barrier, inc=1, **dp_id(mask))

    piece = 16

    def pack(slot, kind, first, count):
        scr = (scr0, scr1)[kind]

        def one(s, carry):
            c = first + s * piece
            rows_in = pl.ds(pl.multiple_of(c * blocks, piece * blocks), piece * blocks)
            stage[slot % groups, kind, pl.ds(c, piece)] = scr[rows_in, :].reshape(piece, blocks, tok).astype(BF16)
            return carry

        lax.fori_loop(0, count // piece, one, 0)

    def send(slot, first, size, sems, ks, kinds=slice(None)):
        there = (slot, kinds, pl.ds(first, size), pl.ds(me * blocks, blocks))
        for k in ks:
            src = stage.at[slot % groups, kinds, pl.ds(mp_peer(k) * blocks + first, size)]
            if k:
                pltpu.make_async_remote_copy(
                    src_ref=src, dst_ref=land.at[there], send_sem=send_sem.at[slot], recv_sem=sems, **mp_id(k)
                ).start()
            else:
                pltpu.make_async_copy(src, land.at[there], sems).start()

    far, near = range(top, mp_ways), range(top)

    def send_all(slot, ks, kinds=slice(None)):
        size = CHUNK if slot == fine_slot else MSG

        def coarse(m):
            send(slot, m * size, size, recv_sem.at[slot * msgs + m], ks, kinds)

        loop(0, fine_first // CHUNK if slot == fine_slot else msgs, coarse)
        if slot == fine_slot:
            for f in range(FINES):
                send(slot, fine_first + f * FINE, FINE, frecv_sem.at[f], ks)

    def sent(slot):
        arrived(stage.at[slot % groups, :, pl.ds(0, (mp_ways - 1) * blocks)], send_sem.at[slot])

    def wait_msg(slot, ch):
        if slot == fine_slot:
            arrived(land.at[slot, :, pl.ds(ch * CHUNK, CHUNK)], recv_sem.at[slot * msgs + ch])
            return

        @pl.when(ch % ratio == 0)
        def _():
            arrived(land.at[slot, :, pl.ds(ch * CHUNK, MSG)], recv_sem.at[slot * msgs + ch // ratio])

    def panel(q, kind, part_of):
        first = part_of * half_width
        cs = slice(first, first + half_width)

        def one(s, carry):
            for u in range(4):
                i = s * 4 + u
                cols = pl.ds(pl.multiple_of(i * width, width), width)
                to = pl.ds(first * blocks + i, half_width, stride=blocks)
                if kind == 0:
                    scr0[to, :] = mm(ur[q, i, :, cs], x[:, cols], 0, 1)
                else:
                    scr1[to, :] = mm(dl[q, i, cs, :], g[:, cols], 1, 1)
            return carry

        lax.fori_loop(0, blocks // 4, one, 0)
        pack(q, kind, first, half_width)

    half = CHUNK // 2
    units = [(0, pl.ds(0, CHUNK), True), (1, pl.ds(0, half), True), (1, pl.ds(half, half), False)]

    def hop_copy(h, src, dst, n, mask):
        pltpu.make_async_remote_copy(
            src_ref=src, dst_ref=dst, send_sem=hop_send.at[h], recv_sem=hop_recv.at[h, n], **dp_id(mask)
        ).start()

    def arrived(ref, sem):
        pltpu.make_async_copy(ref, ref, sem).wait()

    def add_into(ref, at, value):
        ref[at] = (ref[at].astype(F32) + value.astype(F32)).astype(BF16)

    def hop1(n):
        for kind, bl, y_first in units:
            if y_first:
                src = part.at[n, kind, :, :, flip(yb), bl]
            else:
                src = part.at[n, kind, :, flip(zb), :, bl]
            hop_copy(0, src, got1.at[n, kind, :, :, bl], n, 1 if y_first else 2)

    every = slice(None)

    def hop2(n):
        arrived(got1.at[n], hop_recv.at[0, n])
        for kind, bl, y_first in units:
            at = (n, kind, every, every, yb, bl) if y_first else (n, kind, every, zb, every, bl)
            add_into(part, at, got1[n, kind, :, :, bl])
        for kind, bl, y_first in units:
            src = part.at[n, kind, :, flip(zb), yb, bl] if y_first else part.at[n, kind, :, zb, flip(yb), bl]
            hop_copy(1, src, got2.at[n, kind, :, bl], n, 2 if y_first else 1)

    def hop3(n):
        arrived(got2.at[n], hop_recv.at[1, n])
        for kind in range(2):
            add_into(part, (n, kind, every, zb, yb), got2[n, kind])
        hop_copy(2, part.at[n, :, flip(wb), zb, yb], got3.at[n], n, 4)

    def hop_end(n):
        arrived(got3.at[n], hop_recv.at[2, n])
        sums = [(part[n, k, wb, zb, yb].astype(F32) + got3[n, k].astype(F32)) * scale for k in range(2)]
        at = ((n // chunks) % groups, pl.ds((n % chunks) * CHUNK, CHUNK))

        def to_mid():
            gdf[at], gul[at] = sums

        def to_last():
            gdl[at], gur[at] = sums

        if isinstance(n, int):
            (to_mid if n < mid_steps else to_last)()
        else:
            pl.when(n < mid_steps)(to_mid)
            pl.when(n >= mid_steps)(to_last)

    def hops(n):
        for lag, work in zip(LAGS, (hop2, hop3, hop_end)):
            m = n - lag

            @pl.when((m >= 0) & (m < steps))
            def _():
                work(m)

    def fine1(f):
        pltpu.make_async_remote_copy(
            src_ref=fpart.at[f, :, :, :, flip(yb)],
            dst_ref=fgot1.at[f],
            send_sem=fhop_send.at[0],
            recv_sem=fhop_recv.at[0, f],
            **dp_id(1),
        ).start()

    def fine2(f):
        arrived(fgot1.at[f], fhop_recv.at[0, f])
        for kind in range(2):
            add_into(fpart, (f, kind, every, every, yb), fgot1[f, kind])
        for r in (3, 2, 1):
            to_w, to_z = flip(wb) if r >> 1 else wb, flip(zb) if r & 1 else zb
            pltpu.make_async_remote_copy(
                src_ref=fpart.at[f, :, to_w, to_z, yb],
                dst_ref=fgot2.at[f, r - 1],
                send_sem=fhop_send.at[1],
                recv_sem=fhop_recv.at[1, f],
                **dp_id(2 * r),
            ).start()

    def fine_out(f, totals):
        at = (groups - 1, pl.ds(fine_first + f * FINE, FINE))
        for total, out in zip(totals, (gdl, gur)):
            out[at] = total * scale

    def fine_end(f):
        arrived(fgot2.at[f], fhop_recv.at[1, f])
        totals = []
        for kind in range(2):
            total = fpart[f, kind, wb, zb, yb].astype(F32)
            for r in range(3):
                total = total + fgot2[f, r, kind].astype(F32)
            totals.append(total)
        fine_out(f, totals)

    def keep(dst, n, kind, b, value):
        dst[n, kind, :, :, :, b] = value.astype(BF16).reshape(2, 2, 2, rows, width)

    def middle(n, q, c, b):
        w_ul, w_df = ul[q, c], df[q, c]
        cu, dg = land[q, 0, c], land[q, 1, c]
        pre = mm(w_ul, cu, 0, 0)
        sq = pre * pre
        th = jnp.tanh(gelu_root * (pre + gelu_cube * sq * pre))
        part1 = 0.5 * (1.0 + th)
        hidden = (pre * part1).astype(BF16)
        slope = part1 + 0.5 * pre * (1.0 - th * th) * (gelu_root * (1.0 + 3.0 * gelu_cube * sq))
        scr0[pl.ds(c, width, stride=blocks), :] = mm(w_df, hidden, 0, 0)
        pg = (mm(w_df, dg, 1, 0) * slope).astype(BF16)
        scr1[pl.ds(c, width, stride=blocks), :] = mm(w_ul, pg, 1, 0)
        keep(part, n, 0, b, mm(hidden, dg, 1, 1))
        keep(part, n, 1, b, mm(cu, pg, 1, 1))

    def mid_step(q, ch):
        n = q * chunks + ch
        wait_msg(q, ch)
        for b in range(CHUNK):
            middle(n, q, ch * CHUNK + b, b)
        hop1(n)
        hops(n)

    def columns(e):
        return pl.ds(pl.multiple_of(e * width, width), width)

    def last_grads(dst, n, q, e, b):
        cd, rg = land[groups + q, 0, e], land[groups + q, 1, e]
        keep(dst, n, 0, b, mm(cd, g[:, columns(e)], 1, 0))
        keep(dst, n, 1, b, mm(rg, x[:, columns(e)], 1, 0).T)

    def last_outs(q, e):
        cd, rg = land[groups + q, 0, e], land[groups + q, 1, e]
        one = mm(cd, dl[q, e], 0, 0)
        two = mm(ur[q, e], rg, 1, 0)
        if q > 0:
            one, two = one + scr0[columns(e), :], two + scr1[columns(e), :]
        if q < groups - 1:
            scr0[columns(e), :], scr1[columns(e), :] = one, two
        else:
            mixed[:, columns(e)] = one.astype(BF16)
            tgrad[:, columns(e)] = two.T.astype(BF16)

    def last_step(q, ch):
        n = (groups + q) * chunks + ch
        wait_msg(groups + q, ch)
        for b in range(CHUNK):
            last_grads(part, n, q, ch * CHUNK + b, b)
            last_outs(q, ch * CHUNK + b)
        hop1(n)
        hops(n)

    def fine_step(f):
        q = groups - 1
        first = fine_first + f * FINE
        arrived(land.at[fine_slot, :, pl.ds(first, FINE)], frecv_sem.at[f])
        for b in range(FINE):
            last_grads(fpart, f, q, first + b, b)
        fine1(f)
        for b in range(FINE):
            last_outs(q, first + b)

    def loop(start, end, work):
        def one(i, carry):
            work(i)
            return carry

        lax.fori_loop(start, end, one, 0)

    for kind in range(2):
        loads[2 * kind].wait()
        loads[2 * kind + 1].wait()
        for h in range(2):
            pl.when(other == h)(functools.partial(panel, 0, kind, h))
        if kind == 0:
            pl.semaphore_wait(barrier, mp_ways - 1 + len(dp_masks))
        send_all(0, far, kind)
    for kind in range(2):
        for h in range(2):
            pl.when(other != h)(functools.partial(panel, 0, kind, h))
    send_all(0, near)
    for q in range(1, groups):
        for kind in range(2):
            loads[2 + 2 * q + kind].wait()
            for h in range(2):
                panel(q, kind, h)
        send_all(q, [*far, *near])
    loads[-2].wait()
    loads[-1].wait()
    for q in range(groups):
        loop(0, chunks, functools.partial(mid_step, q))
        sent(q)
        for kind in range(2):
            pack(groups + q, kind, 0, width)
        send_all(groups + q, [*far, *near])
    for q in range(groups):
        loop(0, chunks if q < groups - 1 else fine_first // CHUNK, functools.partial(last_step, q))
    fine_step(0)
    hop2(steps - 2)
    hop3(steps - 4)
    hop_end(steps - 6)
    fine_step(1)
    fine_step(2)
    hop2(steps - 1)
    hop3(steps - 3)
    hop_end(steps - 5)
    fine_step(3)
    fine2(0)
    hop3(steps - 2)
    fine2(1)
    hop_end(steps - 4)
    fine2(2)
    hop3(steps - 1)
    fine2(3)
    hop_end(steps - 3)
    fine_end(0)
    hop_end(steps - 2)
    fine_end(1)
    fine_end(2)
    hop_end(steps - 1)
    fine_end(3)
    for q in range(groups):
        sent(groups + q)
    for h, ref in enumerate((got1, got2, got3)):
        arrived(ref, hop_send.at[h])
    for h, ref in enumerate((fgot1, fgot2)):
        arrived(ref, fhop_send.at[h])


def finish_kernel(*refs):
    n = (len(refs) - 1) // 2
    copies = [pltpu.make_async_copy(refs[i], refs[n + i], refs[-1].at[i]) for i in range(n)]
    for c in copies:
        c.start()
    for c in copies:
        c.wait()


def finish(arrays):
    return pl.pallas_call(
        finish_kernel,
        out_shape=[jax.ShapeDtypeStruct(a.shape, a.dtype) for a in arrays],
        in_specs=[VMEM] * len(arrays),
        out_specs=[pl.BlockSpec(memory_space=pl.ANY)] * len(arrays),
        scratch_shapes=[pltpu.SemaphoreType.DMA((len(arrays),))],
        compiler_params=pltpu.CompilerParams(vmem_limit_bytes=16 * 2**20),
    )(*arrays)


def fused(x, g, ur, ul, df, dl, mp_ways):
    groups, blocks, width = ur.shape[0], ur.shape[1], ur.shape[2]
    tok = x.shape[0]
    steps = (2 * groups * blocks - FINES * FINE) // CHUNK
    rows = width // 8
    act = jax.ShapeDtypeStruct(x.shape, BF16)
    grad = jax.ShapeDtypeStruct((groups, blocks, rows, width), F32)
    vm = pltpu.VMEM
    dma = pltpu.SemaphoreType.DMA
    return pl.pallas_call(
        functools.partial(fused_kernel, mp_ways),
        out_shape=[act] * 2 + [grad] * 4,
        in_specs=[HBM] * 6,
        out_specs=[VMEM] * 6,
        scratch_shapes=[
            vm(x.shape, BF16),
            vm(x.shape, BF16),
            vm(ur.shape, BF16),
            vm(ur.shape, BF16),
            vm(ur.shape, BF16),
            vm(ur.shape, BF16),
            vm((width * blocks, tok), F32),
            vm((width * blocks, tok), F32),
            vm((groups, 2, width, blocks, tok), BF16),
            vm((2 * groups, 2, blocks, width, tok), BF16),
            vm((steps, 2, 2, 2, 2, CHUNK, rows, width), BF16),
            vm((steps, 2, 2, 2, CHUNK, rows, width), BF16),
            vm((steps, 2, 2, CHUNK, rows, width), BF16),
            vm((steps, 2, CHUNK, rows, width), BF16),
            vm((FINES, 2, 2, 2, 2, FINE, rows, width), BF16),
            vm((FINES, 2, 2, 2, FINE, rows, width), BF16),
            vm((FINES, 3, 2, FINE, rows, width), BF16),
            dma((2 * groups + 4,)),
            dma((2 * groups,)),
            dma((2 * groups * blocks // MSG + blocks // CHUNK,)),
            dma((FINES,)),
            dma((3,)),
            dma((3, steps)),
            dma((2,)),
            dma((2, FINES)),
        ],
        compiler_params=pltpu.CompilerParams(
            vmem_limit_bytes=49 * 2**20, collective_id=0, has_side_effects=True
        ),
        cost_estimate=pl.CostEstimate(
            flops=48 * groups * blocks * width * width * tok // 2, bytes_accessed=14 * 2**20, transcendentals=0
        ),
    )(x, g, ur, ul, df, dl)


def body(tokens, cotangent, up_right, up_left, down_first_factor, down_left):
    groups, width = up_right.shape[0], up_right.shape[2]
    mp_ways, dp_ways = lax.axis_size("mp"), lax.axis_size("dp")
    if dp_ways == 8 and up_right.shape[1] % 16 == 0:
        return tuple(finish(fused(tokens, cotangent, up_right, up_left, down_first_factor, down_left, mp_ways)))
    scale = (dp_ways * tokens.shape[0]) ** (-0.5)
    me = jnp.stack([lax.axis_index("mp"), lax.axis_index("dp")]).astype(jnp.int32)
    firsts, seconds, reductions = [], [], []
    for q in range(groups):
        firsts.append(exchange(make_panels(me, tokens, cotangent, up_right, down_left, q, mp_ways)))
    for q in range(groups):
        panels, halves = make_middle(me, firsts[q], up_left, down_first_factor, q, dp_ways)
        seconds.append(exchange(panels))
        reductions.append(halves)
    for q in range(groups):
        reductions.append(make_last_grads(me, seconds[q], tokens, cotangent, width, dp_ways))
    sums = halving_rounds(reductions, scale)
    mid_sums, last_sums = sums[:groups], sums[groups:]
    mixed, tokens_grad = make_outputs(me, seconds, down_left, up_right)

    def pick(sums, kind):
        return jnp.stack([s[kind] for s in sums])

    return (mixed, tokens_grad, pick(last_sums, 1), pick(mid_sums, 1), pick(mid_sums, 0), pick(last_sums, 0))


def solution(mesh):
    weight = P(None, "mp", None, None)
    in_specs = (P("dp", "mp"), P("dp", "mp"), weight, weight, weight, weight)
    grad = P(None, "mp", "dp", None)
    out_specs = (P("dp", "mp"), P("dp", "mp"), grad, grad, grad, grad)
    return jax.shard_map(body, mesh=mesh, in_specs=in_specs, out_specs=out_specs, check_vma=False)
```

```python
import functools

import jax
import jax.numpy as jnp
from jax import lax
from jax.experimental import pallas as pl
from jax.experimental.pallas import tpu as pltpu
from jax.sharding import PartitionSpec as P

gelu_root = 0.7978845608
gelu_cube = 0.044715
F32 = jnp.float32
BF16 = jnp.bfloat16


def mm(lhs, rhs, ldim, rdim):
    return lax.dot_general(lhs, rhs, (((ldim,), (rdim,)), ((), ())), preferred_element_type=F32)


def send_panel(outs, kind, scratch, me, blocks):
    span = blocks * blocks
    for k, out in enumerate(outs):
        start = pl.multiple_of((me ^ k) * span, span)
        rows = scratch[pl.ds(start, span), :]
        out[kind] = rows.reshape(out.shape[1:]).astype(BF16)


def gather_rows(parts, kind, scratch, slot, me, block, blocks):
    for k, part in enumerate(parts):
        start = pl.multiple_of((me ^ k) * blocks, blocks)
        scratch[slot, pl.ds(start, blocks), :] = part[kind, block].astype(F32)
    return scratch[slot].astype(BF16)


def hop_order(ways, kind):
    bits = [1 << b for b in range(ways.bit_length() - 1)]
    return [bits[1], bits[0]] + bits[2:] if kind and len(bits) > 1 else bits


def store_grad(outs, kind, block, value, scratch, slot, me, ways):
    rows = value.shape[0] // ways
    first, *later = hop_order(ways, kind)
    scratch[slot] = value
    for p in range(ways // 2):
        rel = sum(bit for t, bit in enumerate(later) if p >> t & 1)
        for out, target in ((outs[2 * kind], rel), (outs[2 * kind + 1], rel + first)):
            start = pl.multiple_of((me ^ target) * rows, rows)
            out[p, block] = scratch[slot, pl.ds(start, rows), :].astype(BF16)


def panels_kernel(ways, me_ref, x_ref, g_ref, ur_ref, dl_ref, *rest):
    outs, scr_r, scr_b = rest[:ways], rest[ways], rest[ways + 1]
    blocks, width = ur_ref.shape[1], ur_ref.shape[2]
    me = me_ref[0]
    for i in range(blocks):
        cols = slice(i * width, (i + 1) * width)
        scr_r[pl.ds(i, width, stride=blocks), :] = mm(ur_ref[0, i], x_ref[:, cols], 0, 1)
        scr_b[pl.ds(i, width, stride=blocks), :] = mm(dl_ref[0, i], g_ref[:, cols], 1, 1)
    send_panel(outs, 0, scr_r, me, blocks)
    send_panel(outs, 1, scr_b, me, blocks)


def full_spec(shape):
    return pl.BlockSpec(shape, lambda s: (0,) * len(shape))


def group_spec(w, q):
    return pl.BlockSpec((1,) + w.shape[1:], lambda s: (q, 0, 0, 0))


def limits(flops, mib):
    return dict(
        compiler_params=pltpu.CompilerParams(vmem_limit_bytes=40 * 2**20),
        cost_estimate=pl.CostEstimate(flops=flops * 8, bytes_accessed=mib * 2**20, transcendentals=0),
    )


def make_panels(me, x, g, ur, dl, q, ways):
    tok, blocks, width = x.shape[0], ur.shape[1], ur.shape[2]
    part = jax.ShapeDtypeStruct((2, blocks, blocks, tok), BF16)
    return pl.pallas_call(
        functools.partial(panels_kernel, ways),
        out_shape=[part] * ways,
        grid=(1,),
        in_specs=[
            pl.BlockSpec(memory_space=pltpu.SMEM),
            full_spec(x.shape),
            full_spec(g.shape),
            group_spec(ur, q),
            group_spec(dl, q),
        ],
        out_specs=[full_spec(part.shape)] * ways,
        scratch_shapes=[pltpu.VMEM((width * blocks, tok), F32)] * 2,
        **limits(4 * tok * blocks * width * width, 8),
    )(me, x, g, ur, dl)


UNROLL = 4


def middle_kernel(mp_ways, dp_ways, me_ref, ul_ref, df_ref, *rest):
    n = mp_ways
    first_in, outs, grads = rest[:n], rest[n : 2 * n], rest[2 * n : 2 * n + 4]
    scr_d, scr_u, asm_r, asm_b, gr1, gr2 = rest[2 * n + 4 :]
    blocks, width = ul_ref.shape[1], ul_ref.shape[2]
    me_mp, me_dp = me_ref[0], me_ref[1]

    def one(c, slot):
        ul, df = ul_ref[0, c], df_ref[0, c]
        cu = gather_rows(first_in, 0, asm_r, slot, me_mp, c, blocks)
        dg = gather_rows(first_in, 1, asm_b, slot, me_mp, c, blocks)
        pre = mm(ul, cu, 0, 0)
        sq = pre * pre
        th = jnp.tanh(gelu_root * (pre + gelu_cube * sq * pre))
        half = 0.5 * (1.0 + th)
        hidden = (pre * half).astype(BF16)
        slope = half + 0.5 * pre * (1.0 - th * th) * (gelu_root * (1.0 + 3.0 * gelu_cube * sq))
        scr_d[pl.ds(c, width, stride=blocks), :] = mm(df, hidden, 0, 0)
        pg = (mm(df, dg, 1, 0) * slope).astype(BF16)
        scr_u[pl.ds(c, width, stride=blocks), :] = mm(ul, pg, 1, 0)
        store_grad(grads, 0, c, mm(hidden, dg, 1, 1), gr1, slot, me_dp, dp_ways)
        store_grad(grads, 1, c, mm(cu, pg, 1, 1), gr2, slot, me_dp, dp_ways)

    def step(s, carry):
        for slot in range(UNROLL):
            one(s * UNROLL + slot, slot)
        return carry

    lax.fori_loop(0, blocks // UNROLL, step, 0)
    send_panel(outs, 0, scr_d, me_mp, blocks)
    send_panel(outs, 1, scr_u, me_mp, blocks)


def grad_halves(blocks, width, dp_ways):
    return jax.ShapeDtypeStruct((dp_ways // 2, blocks, width // dp_ways, width), BF16)


def make_middle(me, first_in, ul, df, q, dp_ways):
    n = len(first_in)
    part = jax.ShapeDtypeStruct(first_in[0].shape, BF16)
    blocks, width, tok = ul.shape[1], ul.shape[2], part.shape[3]
    half = grad_halves(blocks, width, dp_ways)
    res = pl.pallas_call(
        functools.partial(middle_kernel, n, dp_ways),
        out_shape=[part] * n + [half] * 4,
        grid=(1,),
        in_specs=[pl.BlockSpec(memory_space=pltpu.SMEM)] + [group_spec(ul, q)] * 2 + [full_spec(part.shape)] * n,
        out_specs=[full_spec(part.shape)] * n + [full_spec(half.shape)] * 4,
        scratch_shapes=[pltpu.VMEM((width * blocks, tok), F32)] * 2
        + [pltpu.VMEM((UNROLL, width, tok), F32)] * 2
        + [pltpu.VMEM((UNROLL, width, width), F32)] * 2,
        **limits(12 * tok * blocks * width * width, 8),
    )(me, ul, df, *first_in)
    return res[:n], res[n:]


def last_grads_kernel(mp_ways, dp_ways, me_ref, x_ref, g_ref, *rest):
    n = mp_ways
    second_in, grads = rest[:n], rest[n : n + 4]
    asm_d, asm_u, gr1, gr2 = rest[n + 4 :]
    blocks = second_in[0].shape[1]
    width = gr1.shape[1]
    me_mp, me_dp = me_ref[0], me_ref[1]
    for e in range(blocks):
        cols = slice(e * width, (e + 1) * width)
        slot = e % UNROLL
        cd = gather_rows(second_in, 0, asm_d, slot, me_mp, e, blocks)
        rg = gather_rows(second_in, 1, asm_u, slot, me_mp, e, blocks)
        store_grad(grads, 0, e, mm(cd, g_ref[:, cols], 1, 0), gr1, slot, me_dp, dp_ways)
        store_grad(grads, 1, e, mm(rg, x_ref[:, cols], 1, 0).T, gr2, slot, me_dp, dp_ways)


def make_last_grads(me, second_in, x, g, width, dp_ways):
    n = len(second_in)
    part = second_in[0]
    blocks, tok = part.shape[1], part.shape[3]
    half = grad_halves(blocks, width, dp_ways)
    return pl.pallas_call(
        functools.partial(last_grads_kernel, n, dp_ways),
        out_shape=[half] * 4,
        grid=(1,),
        in_specs=[pl.BlockSpec(memory_space=pltpu.SMEM)] + [full_spec(x.shape)] * 2 + [full_spec(part.shape)] * n,
        out_specs=[full_spec(half.shape)] * 4,
        scratch_shapes=[pltpu.VMEM((UNROLL, width, tok), F32)] * 2 + [pltpu.VMEM((UNROLL, width, width), F32)] * 2,
        **limits(4 * tok * blocks * width * width, 6),
    )(me, x, g, *second_in)


def outputs_kernel(mp_ways, me_ref, dl_ref, ur_ref, *rest):
    n = mp_ways
    groups = dl_ref.shape[0]
    second_in = rest[: groups * n]
    mixed, tgrad, asm_d, asm_u = rest[groups * n :]
    blocks, width = dl_ref.shape[1], dl_ref.shape[2]
    me_mp = me_ref[0]
    for e in range(blocks):
        cols = slice(e * width, (e + 1) * width)
        out_sum = grad_sum = None
        for q in range(groups):
            parts = second_in[q * n : (q + 1) * n]
            slot = (e * groups + q) % UNROLL
            cd = gather_rows(parts, 0, asm_d, slot, me_mp, e, blocks)
            rg = gather_rows(parts, 1, asm_u, slot, me_mp, e, blocks)
            one = mm(cd, dl_ref[q, e], 0, 0)
            two = mm(ur_ref[q, e], rg, 1, 0)
            out_sum = one if q == 0 else out_sum + one
            grad_sum = two if q == 0 else grad_sum + two
        mixed[:, cols] = out_sum.astype(BF16)
        tgrad[:, cols] = grad_sum.T.astype(BF16)


def make_outputs(me, second_in, dl, ur):
    n = len(second_in[0])
    part = second_in[0][0]
    groups, blocks, width, tok = dl.shape[0], dl.shape[1], dl.shape[2], part.shape[3]
    out = jax.ShapeDtypeStruct((tok, blocks * width), BF16)
    return pl.pallas_call(
        functools.partial(outputs_kernel, n),
        out_shape=[out] * 2,
        grid=(1,),
        in_specs=[pl.BlockSpec(memory_space=pltpu.SMEM)]
        + [full_spec(dl.shape)] * 2
        + [full_spec(part.shape)] * (n * groups),
        out_specs=[full_spec(out.shape)] * 2,
        scratch_shapes=[pltpu.VMEM((UNROLL, width, tok), F32)] * 2,
        **limits(8 * tok * blocks * width * width, 10),
    )(me, dl, ur, *[p for parts in second_in for p in parts])


def xor_permute(array, axis, k):
    return lax.ppermute(array, axis, [(i, i ^ k) for i in range(lax.axis_size(axis))])


def exchange(parts):
    return [p if k == 0 else xor_permute(p, "mp", k) for k, p in enumerate(parts)]


def halving_rounds(reductions, scale):
    ways = lax.axis_size("dp")
    orders = [hop_order(ways, kind) for kind in range(2)]
    hops = len(orders[0])
    pairs = [[[h[0], h[1]], [h[2], h[3]]] for h in reductions]
    sums = [[None, None] for _ in reductions]
    for turn in range(hops + len(reductions) - 1):
        active = [(s, kind) for s in range(len(reductions)) if 0 <= turn - s < hops for kind in range(2)]
        got = [xor_permute(pairs[s][kind][1], "dp", orders[kind][turn - s]) for s, kind in active]
        got = lax.optimization_barrier(got)
        for (s, kind), arrived in zip(active, got):
            total = pairs[s][kind][0].astype(F32) + arrived.astype(F32)
            if total.shape[0] == 1:
                sums[s][kind] = total[0] * scale
                continue
            total = total.astype(BF16).reshape((total.shape[0] // 2, 2) + total.shape[1:])
            pairs[s][kind] = [total[:, 0], total[:, 1]]
    return sums


MSG = 8
CHUNK = 4
FINE = 1
FINES = 4
LAGS = (2, 4, 6)
MESH_IDS = pl.DeviceIdType.MESH
HBM = pl.BlockSpec(memory_space=pltpu.HBM)
VMEM = pl.BlockSpec(memory_space=pltpu.VMEM)


def flip(v):
    return 1 - v


def fused_kernel(
    mp_ways,
    x_in,
    g_in,
    ur_in,
    ul_in,
    df_in,
    dl_in,
    mixed,
    tgrad,
    gur,
    gul,
    gdf,
    gdl,
    x,
    g,
    ur,
    ul,
    df,
    dl,
    scr0,
    scr1,
    stage,
    land,
    part,
    got1,
    got2,
    got3,
    fpart,
    fgot1,
    fgot2,
    in_sem,
    send_sem,
    recv_sem,
    frecv_sem,
    hop_send,
    hop_recv,
    fhop_send,
    fhop_recv,
):
    groups, blocks, width = ur.shape[0], ur.shape[1], ur.shape[2]
    tok = x.shape[0]
    chunks, msgs, ratio = blocks // CHUNK, blocks // MSG, MSG // CHUNK
    fine_first = blocks - FINES * FINE
    rows = width // 8
    half_width = width // 2
    fine_slot = 2 * groups - 1
    steps = fine_slot * chunks + fine_first // CHUNK
    mid_steps = groups * chunks
    scale = (8 * tok) ** (-0.5)
    me, dp = lax.axis_index("mp"), lax.axis_index("dp")
    yb, zb, wb = dp % 2, (dp // 2) % 2, dp // 4
    top = mp_ways // 2
    other = flip(me // top)

    def mp_peer(k):
        total = 0
        for b in range(mp_ways.bit_length() - 1):
            bit = (me // (1 << b)) % 2
            total = total + (flip(bit) if k >> b & 1 else bit) * (1 << b)
        return total

    def dp_peer(mask):
        peer = dp
        for b in range(3):
            if mask >> b & 1:
                peer = peer + (1 - 2 * ((dp // (1 << b)) % 2)) * (1 << b)
        return peer

    def mp_id(k):
        return dict(device_id={"mp": mp_peer(k)}, device_id_type=MESH_IDS)

    def dp_id(mask):
        return dict(device_id={"dp": dp_peer(mask)}, device_id_type=MESH_IDS)

    loads = [(x_in, x), (ur_in.at[0], ur.at[0]), (g_in, g), (dl_in.at[0], dl.at[0])]
    for q in range(1, groups):
        loads += [(ur_in.at[q], ur.at[q]), (dl_in.at[q], dl.at[q])]
    loads += [(ul_in, ul), (df_in, df)]
    loads = [pltpu.make_async_copy(a, b, in_sem.at[i]) for i, (a, b) in enumerate(loads)]
    for c in loads:
        c.start()

    barrier = pltpu.get_barrier_semaphore()
    dp_masks = (1, 2, 4, 6)
    for k in range(1, mp_ways):
        pl.semaphore_signal(barrier, inc=1, **mp_id(k))
    for mask in dp_masks:
        pl.semaphore_signal(barrier, inc=1, **dp_id(mask))

    piece = 16

    def pack(slot, kind, first, count):
        scr = (scr0, scr1)[kind]

        def one(s, carry):
            c = first + s * piece
            rows_in = pl.ds(pl.multiple_of(c * blocks, piece * blocks), piece * blocks)
            stage[slot % groups, kind, pl.ds(c, piece)] = scr[rows_in, :].reshape(piece, blocks, tok).astype(BF16)
            return carry

        lax.fori_loop(0, count // piece, one, 0)

    def send(slot, first, size, sems, ks, kinds=slice(None)):
        there = (slot, kinds, pl.ds(first, size), pl.ds(me * blocks, blocks))
        for k in ks:
            src = stage.at[slot % groups, kinds, pl.ds(mp_peer(k) * blocks + first, size)]
            if k:
                pltpu.make_async_remote_copy(
                    src_ref=src, dst_ref=land.at[there], send_sem=send_sem.at[slot], recv_sem=sems, **mp_id(k)
                ).start()
            else:
                pltpu.make_async_copy(src, land.at[there], sems).start()

    far, near = range(top, mp_ways), range(top)

    def send_all(slot, ks, kinds=slice(None)):
        size = CHUNK if slot == fine_slot else MSG

        def coarse(m):
            send(slot, m * size, size, recv_sem.at[slot * msgs + m], ks, kinds)

        loop(0, fine_first // CHUNK if slot == fine_slot else msgs, coarse)
        if slot == fine_slot:
            for f in range(FINES):
                send(slot, fine_first + f * FINE, FINE, frecv_sem.at[f], ks)

    def sent(slot):
        arrived(stage.at[slot % groups, :, pl.ds(0, (mp_ways - 1) * blocks)], send_sem.at[slot])

    def wait_msg(slot, ch):
        if slot == fine_slot:
            arrived(land.at[slot, :, pl.ds(ch * CHUNK, CHUNK)], recv_sem.at[slot * msgs + ch])
            return

        @pl.when(ch % ratio == 0)
        def _():
            arrived(land.at[slot, :, pl.ds(ch * CHUNK, MSG)], recv_sem.at[slot * msgs + ch // ratio])

    def panel(q, kind, part_of):
        first = part_of * half_width
        cs = slice(first, first + half_width)

        def one(s, carry):
            for u in range(8):
                i = s * 8 + u
                cols = pl.ds(pl.multiple_of(i * width, width), width)
                to = pl.ds(first * blocks + i, half_width, stride=blocks)
                if kind == 0:
                    scr0[to, :] = mm(ur[q, i, :, cs], x[:, cols], 0, 1)
                else:
                    scr1[to, :] = mm(dl[q, i, cs, :], g[:, cols], 1, 1)
            return carry

        lax.fori_loop(0, blocks // 8, one, 0)
        pack(q, kind, first, half_width)

    half = CHUNK // 2
    units = [(0, pl.ds(0, CHUNK), True), (1, pl.ds(0, half), True), (1, pl.ds(half, half), False)]

    def hop_copy(h, src, dst, n, mask):
        pltpu.make_async_remote_copy(
            src_ref=src, dst_ref=dst, send_sem=hop_send.at[h], recv_sem=hop_recv.at[h, n], **dp_id(mask)
        ).start()

    def arrived(ref, sem):
        pltpu.make_async_copy(ref, ref, sem).wait()

    def add_into(ref, at, value):
        ref[at] = (ref[at].astype(F32) + value.astype(F32)).astype(BF16)

    def hop1(n):
        for kind, bl, y_first in units:
            if y_first:
                src = part.at[n, kind, :, :, flip(yb), bl]
            else:
                src = part.at[n, kind, :, flip(zb), :, bl]
            hop_copy(0, src, got1.at[n, kind, :, :, bl], n, 1 if y_first else 2)

    every = slice(None)

    def hop2(n):
        arrived(got1.at[n], hop_recv.at[0, n])
        for kind, bl, y_first in units:
            at = (n, kind, every, every, yb, bl) if y_first else (n, kind, every, zb, every, bl)
            add_into(part, at, got1[n, kind, :, :, bl])
        for kind, bl, y_first in units:
            src = part.at[n, kind, :, flip(zb), yb, bl] if y_first else part.at[n, kind, :, zb, flip(yb), bl]
            hop_copy(1, src, got2.at[n, kind, :, bl], n, 2 if y_first else 1)

    def hop3(n):
        arrived(got2.at[n], hop_recv.at[1, n])
        for kind in range(2):
            add_into(part, (n, kind, every, zb, yb), got2[n, kind])
        hop_copy(2, part.at[n, :, flip(wb), zb, yb], got3.at[n], n, 4)

    def hop_end(n):
        arrived(got3.at[n], hop_recv.at[2, n])
        sums = [(part[n, k, wb, zb, yb].astype(F32) + got3[n, k].astype(F32)) * scale for k in range(2)]
        at = ((n // chunks) % groups, pl.ds((n % chunks) * CHUNK, CHUNK))

        def to_mid():
            gdf[at], gul[at] = sums

        def to_last():
            gdl[at], gur[at] = sums

        if isinstance(n, int):
            (to_mid if n < mid_steps else to_last)()
        else:
            pl.when(n < mid_steps)(to_mid)
            pl.when(n >= mid_steps)(to_last)

    def hops(n):
        for lag, work in zip(LAGS, (hop2, hop3, hop_end)):
            m = n - lag

            @pl.when((m >= 0) & (m < steps))
            def _():
                work(m)

    def fine1(f):
        pltpu.make_async_remote_copy(
            src_ref=fpart.at[f, :, :, :, flip(yb)],
            dst_ref=fgot1.at[f],
            send_sem=fhop_send.at[0],
            recv_sem=fhop_recv.at[0, f],
            **dp_id(1),
        ).start()

    def fine2(f):
        arrived(fgot1.at[f], fhop_recv.at[0, f])
        for kind in range(2):
            add_into(fpart, (f, kind, every, every, yb), fgot1[f, kind])
        for r in (3, 2, 1):
            to_w, to_z = flip(wb) if r >> 1 else wb, flip(zb) if r & 1 else zb
            pltpu.make_async_remote_copy(
                src_ref=fpart.at[f, :, to_w, to_z, yb],
                dst_ref=fgot2.at[f, r - 1],
                send_sem=fhop_send.at[1],
                recv_sem=fhop_recv.at[1, f],
                **dp_id(2 * r),
            ).start()

    def fine_out(f, totals):
        at = (groups - 1, pl.ds(fine_first + f * FINE, FINE))
        for total, out in zip(totals, (gdl, gur)):
            out[at] = total * scale

    def fine_end(f):
        arrived(fgot2.at[f], fhop_recv.at[1, f])
        totals = []
        for kind in range(2):
            total = fpart[f, kind, wb, zb, yb].astype(F32)
            for r in range(3):
                total = total + fgot2[f, r, kind].astype(F32)
            totals.append(total)
        fine_out(f, totals)

    def keep(dst, n, kind, b, value):
        dst[n, kind, :, :, :, b] = value.astype(BF16).reshape(2, 2, 2, rows, width)

    def middle(n, q, c, b):
        w_ul, w_df = ul[q, c], df[q, c]
        cu, dg = land[q, 0, c], land[q, 1, c]
        pre = mm(w_ul, cu, 0, 0)
        sq = pre * pre
        th = jnp.tanh(gelu_root * (pre + gelu_cube * sq * pre))
        part1 = 0.5 * (1.0 + th)
        hidden = (pre * part1).astype(BF16)
        slope = part1 + 0.5 * pre * (1.0 - th * th) * (gelu_root * (1.0 + 3.0 * gelu_cube * sq))
        scr0[pl.ds(c, width, stride=blocks), :] = mm(w_df, hidden, 0, 0)
        pg = (mm(w_df, dg, 1, 0) * slope).astype(BF16)
        scr1[pl.ds(c, width, stride=blocks), :] = mm(w_ul, pg, 1, 0)
        keep(part, n, 0, b, mm(hidden, dg, 1, 1))
        keep(part, n, 1, b, mm(cu, pg, 1, 1))

    def mid_step(q, ch):
        n = q * chunks + ch
        wait_msg(q, ch)
        for b in range(CHUNK):
            middle(n, q, ch * CHUNK + b, b)
        hop1(n)
        hops(n)

    def columns(e):
        return pl.ds(pl.multiple_of(e * width, width), width)

    def last_grads(dst, n, q, e, b):
        cd, rg = land[groups + q, 0, e], land[groups + q, 1, e]
        keep(dst, n, 0, b, mm(cd, g[:, columns(e)], 1, 0))
        keep(dst, n, 1, b, mm(rg, x[:, columns(e)], 1, 0).T)

    def last_outs(q, e):
        cd, rg = land[groups + q, 0, e], land[groups + q, 1, e]
        one = mm(cd, dl[q, e], 0, 0)
        two = mm(ur[q, e], rg, 1, 0)
        if q > 0:
            one, two = one + scr0[columns(e), :], two + scr1[columns(e), :]
        if q < groups - 1:
            scr0[columns(e), :], scr1[columns(e), :] = one, two
        else:
            mixed[:, columns(e)] = one.astype(BF16)
            tgrad[:, columns(e)] = two.T.astype(BF16)

    def last_step(q, ch):
        n = (groups + q) * chunks + ch
        wait_msg(groups + q, ch)
        for b in range(CHUNK):
            last_grads(part, n, q, ch * CHUNK + b, b)
            last_outs(q, ch * CHUNK + b)
        hop1(n)
        hops(n)

    def fine_step(f):
        q = groups - 1
        first = fine_first + f * FINE
        arrived(land.at[fine_slot, :, pl.ds(first, FINE)], frecv_sem.at[f])
        for b in range(FINE):
            last_grads(fpart, f, q, first + b, b)
        fine1(f)
        for b in range(FINE):
            last_outs(q, first + b)

    def loop(start, end, work):
        def one(i, carry):
            work(i)
            return carry

        lax.fori_loop(start, end, one, 0)

    for kind in range(2):
        loads[2 * kind].wait()
        loads[2 * kind + 1].wait()
        for h in range(2):
            pl.when(other == h)(functools.partial(panel, 0, kind, h))
        if kind == 0:
            pl.semaphore_wait(barrier, mp_ways - 1 + len(dp_masks))
        send_all(0, far, kind)
    for kind in range(2):
        for h in range(2):
            pl.when(other != h)(functools.partial(panel, 0, kind, h))
    send_all(0, near)
    for q in range(1, groups):
        for kind in range(2):
            loads[2 + 2 * q + kind].wait()
            for h in range(2):
                panel(q, kind, h)
        send_all(q, [*far, *near])
    loads[-2].wait()
    loads[-1].wait()
    for q in range(groups):
        loop(0, chunks, functools.partial(mid_step, q))
        sent(q)
        for kind in range(2):
            pack(groups + q, kind, 0, width)
        send_all(groups + q, [*far, *near])
    for q in range(groups):
        loop(0, chunks if q < groups - 1 else fine_first // CHUNK, functools.partial(last_step, q))
    fine_step(0)
    hop2(steps - 2)
    hop3(steps - 4)
    hop_end(steps - 6)
    fine_step(1)
    fine_step(2)
    hop2(steps - 1)
    hop3(steps - 3)
    hop_end(steps - 5)
    fine_step(3)
    fine2(0)
    hop3(steps - 2)
    fine2(1)
    hop_end(steps - 4)
    fine2(2)
    hop3(steps - 1)
    fine2(3)
    hop_end(steps - 3)
    fine_end(0)
    hop_end(steps - 2)
    fine_end(1)
    fine_end(2)
    hop_end(steps - 1)
    fine_end(3)
    for q in range(groups):
        sent(groups + q)
    for h, ref in enumerate((got1, got2, got3)):
        arrived(ref, hop_send.at[h])
    for h, ref in enumerate((fgot1, fgot2)):
        arrived(ref, fhop_send.at[h])


def finish_kernel(*refs):
    n = (len(refs) - 1) // 2
    copies = [pltpu.make_async_copy(refs[i], refs[n + i], refs[-1].at[i]) for i in range(n)]
    for c in copies:
        c.start()
    for c in copies:
        c.wait()


def finish(arrays):
    return pl.pallas_call(
        finish_kernel,
        out_shape=[jax.ShapeDtypeStruct(a.shape, a.dtype) for a in arrays],
        in_specs=[VMEM] * len(arrays),
        out_specs=[pl.BlockSpec(memory_space=pl.ANY)] * len(arrays),
        scratch_shapes=[pltpu.SemaphoreType.DMA((len(arrays),))],
        compiler_params=pltpu.CompilerParams(vmem_limit_bytes=16 * 2**20),
    )(*arrays)


def fused(x, g, ur, ul, df, dl, mp_ways):
    groups, blocks, width = ur.shape[0], ur.shape[1], ur.shape[2]
    tok = x.shape[0]
    steps = (2 * groups * blocks - FINES * FINE) // CHUNK
    rows = width // 8
    act = jax.ShapeDtypeStruct(x.shape, BF16)
    grad = jax.ShapeDtypeStruct((groups, blocks, rows, width), F32)
    vm = pltpu.VMEM
    dma = pltpu.SemaphoreType.DMA
    return pl.pallas_call(
        functools.partial(fused_kernel, mp_ways),
        out_shape=[act] * 2 + [grad] * 4,
        in_specs=[HBM] * 6,
        out_specs=[VMEM] * 6,
        scratch_shapes=[
            vm(x.shape, BF16),
            vm(x.shape, BF16),
            vm(ur.shape, BF16),
            vm(ur.shape, BF16),
            vm(ur.shape, BF16),
            vm(ur.shape, BF16),
            vm((width * blocks, tok), F32),
            vm((width * blocks, tok), F32),
            vm((groups, 2, width, blocks, tok), BF16),
            vm((2 * groups, 2, blocks, width, tok), BF16),
            vm((steps, 2, 2, 2, 2, CHUNK, rows, width), BF16),
            vm((steps, 2, 2, 2, CHUNK, rows, width), BF16),
            vm((steps, 2, 2, CHUNK, rows, width), BF16),
            vm((steps, 2, CHUNK, rows, width), BF16),
            vm((FINES, 2, 2, 2, 2, FINE, rows, width), BF16),
            vm((FINES, 2, 2, 2, FINE, rows, width), BF16),
            vm((FINES, 3, 2, FINE, rows, width), BF16),
            dma((2 * groups + 4,)),
            dma((2 * groups,)),
            dma((2 * groups * blocks // MSG + blocks // CHUNK,)),
            dma((FINES,)),
            dma((3,)),
            dma((3, steps)),
            dma((2,)),
            dma((2, FINES)),
        ],
        compiler_params=pltpu.CompilerParams(
            vmem_limit_bytes=49 * 2**20, collective_id=0, has_side_effects=True
        ),
        cost_estimate=pl.CostEstimate(
            flops=48 * groups * blocks * width * width * tok // 2, bytes_accessed=14 * 2**20, transcendentals=0
        ),
    )(x, g, ur, ul, df, dl)


def body(tokens, cotangent, up_right, up_left, down_first_factor, down_left):
    groups, width = up_right.shape[0], up_right.shape[2]
    mp_ways, dp_ways = lax.axis_size("mp"), lax.axis_size("dp")
    if dp_ways == 8 and up_right.shape[1] % 16 == 0:
        return tuple(finish(fused(tokens, cotangent, up_right, up_left, down_first_factor, down_left, mp_ways)))
    scale = (dp_ways * tokens.shape[0]) ** (-0.5)
    me = jnp.stack([lax.axis_index("mp"), lax.axis_index("dp")]).astype(jnp.int32)
    firsts, seconds, reductions = [], [], []
    for q in range(groups):
        firsts.append(exchange(make_panels(me, tokens, cotangent, up_right, down_left, q, mp_ways)))
    for q in range(groups):
        panels, halves = make_middle(me, firsts[q], up_left, down_first_factor, q, dp_ways)
        seconds.append(exchange(panels))
        reductions.append(halves)
    for q in range(groups):
        reductions.append(make_last_grads(me, seconds[q], tokens, cotangent, width, dp_ways))
    sums = halving_rounds(reductions, scale)
    mid_sums, last_sums = sums[:groups], sums[groups:]
    mixed, tokens_grad = make_outputs(me, seconds, down_left, up_right)

    def pick(sums, kind):
        return jnp.stack([s[kind] for s in sums])

    return (mixed, tokens_grad, pick(last_sums, 1), pick(mid_sums, 1), pick(mid_sums, 0), pick(last_sums, 0))


def solution(mesh):
    weight = P(None, "mp", None, None)
    in_specs = (P("dp", "mp"), P("dp", "mp"), weight, weight, weight, weight)
    grad = P(None, "mp", "dp", None)
    out_specs = (P("dp", "mp"), P("dp", "mp"), grad, grad, grad, grad)
    return jax.shard_map(body, mesh=mesh, in_specs=in_specs, out_specs=out_specs, check_vma=False)
```
